32 devices in a mesh: grp: 1, date: 4 (over y, x), shard: 8 (over z, core).
Axes of the slice: x: 2, y: 2, z: 4, core: 2. Of those that a mesh axis runs over, the one named last changes fastest.
Arguments:
- echo_spectra: bfloat16 [4, 2, 128, 8192], P(('grp', 'date'), None, 'shard'), may hold values from -6 to 6
- range_reference: float32 [2, 8192], replicated, may hold values from -5 to 5
- azimuth_reference: bfloat16 [2, 128, 8192], P(None, None, 'shard'), may hold values from -5 to 5
- block_owner: int32 [4, 64], P(('grp', 'date')), may hold values from 0 to 7, as said below
- block_slot: int32 [4, 64], P(('grp', 'date')), may hold values from 0 to 15, as said below
- kernel_index: int32 [4, 64], P(('grp', 'date')), may hold values from 0 to 7
Outputs:
- filtered: bfloat16 [4, 128, 2, 2, 128, 128], P(('grp', 'date'), 'shard')
The draws below stay inside these ranges and needn't reach their ends.
Inputs may be any that keep to these rules, and one draw needn't show every extreme that they name: `block_owner`: every date carries the same owners (the stack is coregistered onto one map grid). Within a date, the 8 blocks of one range-column group name any one owner at most 2 times, and some group names some owner exactly 2 times; every owner is named by at most 16 blocks, and some owner by exactly 16. `block_slot`: every date carries the same slots. Within a date, blocks that name the same owner have distinct slots.
All inputs are finite; a program needn't handle non-finite values.
Results may differ from the reference program's by a relative error of at most 0.017.
Values may be sent and summed in bfloat16 or wider, within the bound.
A program may use at most 128 MiB of HBM per device.

```python
import math
import jax
import jax.numpy as jnp
from jax import lax

RNG = 8192
RSPLIT = 64
BLK = 128
NSUB = 8
DATES = 4
PULSES = 128
BLK_DEV = 8
BLOCKS = 64
MOST = 2
CAP = 16
TILES = 128
N_SHARD = 8


def slot_shuffle(perm_key):
    return jax.random.permutation(perm_key, CAP).astype(jnp.int32)


def local_shuffle(perm_key):
    return jax.random.permutation(perm_key, BLK_DEV).astype(jnp.int32)


def plan_grid(grid_key):
    keys = jax.random.split(grid_key, 4)
    extra = CAP - BLK_DEV
    swing = jax.random.randint(keys[0], (N_SHARD // 2,), 0, extra + 1).astype(jnp.int32)
    swing = swing.at[0].set(extra)
    loads = jnp.stack([BLK_DEV + swing, BLK_DEV - swing], axis=1).reshape(N_SHARD)
    order = jax.random.permutation(keys[1], N_SHARD).astype(jnp.int32)
    ends = jnp.cumsum(loads).astype(jnp.int32)
    starts = ends - loads
    place = jnp.arange(BLOCKS, dtype=jnp.int32)
    segment = jnp.sum((place[:, None] >= ends[None, :]).astype(jnp.int32), axis=1)
    owner = order[segment]
    rank = place - starts[segment]
    sender = place // MOST % N_SHARD
    local = place // (MOST * N_SHARD) * MOST + place % MOST
    slot_perms = jax.vmap(slot_shuffle)(jax.random.split(keys[2], N_SHARD))
    slot = slot_perms[owner, rank]
    local_perms = jax.vmap(local_shuffle)(jax.random.split(keys[3], N_SHARD))
    target = sender * BLK_DEV + local_perms[sender, local]
    owners = jnp.zeros((BLOCKS,), jnp.int32).at[target].set(owner)
    slots = jnp.zeros((BLOCKS,), jnp.int32).at[target].set(slot)
    return (owners, slots)


def block_plan(key):
    base = jax.random.fold_in(key, 11)
    owners, slots = plan_grid(base)
    return (jnp.broadcast_to(owners[None, :], (DATES, BLOCKS)), jnp.broadcast_to(slots[None, :], (DATES, BLOCKS)))


def draw_block_owner(key, part):
    return block_plan(key)[0]


def draw_block_slot(key, part):
    return block_plan(key)[1]


def with_ends(array, rng, least, high):
    index_at = [jax.random.randint(jax.random.fold_in(rng, axis), (), 0, length) for axis, length in enumerate(array.shape)]
    widest = array.shape.index(max(array.shape))
    neighbour = index_at[:widest] + [(index_at[widest] + 1) % array.shape[widest]] + index_at[widest + 1:]
    return array.at[tuple(index_at)].set(least).at[tuple(neighbour)].set(high)


def shard_levels(key, dims, pieces, smallest, top_value):
    level = 1.0
    for axis_at, blocks in pieces:
        draws = jax.random.uniform(jax.random.fold_in(jax.random.fold_in(key, 6), axis_at), (blocks,), jnp.float32, smallest / len(pieces), top_value / len(pieces))
        level = level * jnp.repeat(jnp.exp(draws), dims[axis_at] // blocks).reshape((-1,) + (1,) * (len(dims) - 1 - axis_at))
    return level


def gaussian(key, dims, deviation, limit, pieces=(), held_as=jnp.bfloat16):
    result = deviation * jax.random.normal(key, dims, jnp.float32)
    if pieces:
        result = result * shard_levels(key, dims, pieces, -0.22, 0.18)
    return jnp.clip(result, -limit, limit).astype(held_as)


def setup_inputs(seed: int = 0, part: int = 0) -> dict:
    key_of = jax.random.split(jax.random.key(seed), 7)
    part_keys = jax.random.split(jax.random.fold_in(key_of[6], part), 7)
    echo_spectra = gaussian(part_keys[0], (DATES, 2, PULSES, RNG), 1.0, 6.0, ((0, 4), (2, 8)))
    range_reference = gaussian(key_of[1], (2, RNG), 0.7, 5.0, (), jnp.float32)
    azimuth_reference = gaussian(key_of[2], (2, PULSES, RNG), 0.7, 5.0, ((2, 8),))
    block_owner = draw_block_owner(jax.random.fold_in(jax.random.fold_in(key_of[6], part), 71), part)
    block_slot = draw_block_slot(jax.random.fold_in(jax.random.fold_in(key_of[6], part), 71), part)
    kernel_index = with_ends(jax.random.randint(part_keys[5], (DATES, BLOCKS), 0, NSUB), jax.random.fold_in(part_keys[5], 1), 0, NSUB - 1).astype(jnp.int32)
    return {"echo_spectra": echo_spectra, "range_reference": range_reference, "azimuth_reference": azimuth_reference, "block_owner": block_owner, "block_slot": block_slot, "kernel_index": kernel_index}


def dft_block(size, sign):
    index = jnp.arange(size, dtype=jnp.int32)
    phase = index[:, None] * index[None, :] % size
    angle = 2.0 * math.pi / size * phase.astype(jnp.float32)
    scale = 1.0 / math.sqrt(size)
    cosine = jnp.cos(angle) * scale
    sine = sign * jnp.sin(angle) * scale
    table = jnp.stack([jnp.stack([cosine, -sine]), jnp.stack([sine, cosine])])
    return jnp.transpose(table, (0, 2, 1, 3)).astype(jnp.bfloat16)

def twiddle(first_len, second_len, total):
    left = jnp.arange(first_len, dtype=jnp.int32)
    right = jnp.arange(second_len, dtype=jnp.int32)
    phase = left[:, None] * right[None, :] % total
    angle = 2.0 * math.pi / total * phase.astype(jnp.float32)
    return (jnp.cos(angle), jnp.sin(angle))

def kernel_table():
    offset = (jnp.arange(NSUB, dtype=jnp.float32) + 0.5) / NSUB
    cells = jnp.arange(BLK, dtype=jnp.float32)
    dist = cells[None, None, :] - cells[None, :, None] - offset[:, None, None]
    window = jnp.where(jnp.abs(dist) < 4.0, 0.5 + 0.5 * jnp.cos(math.pi * dist / 4.0), 0.0)
    return (jnp.sinc(dist) * window).astype(jnp.bfloat16)

def fdot(form, left, right):
    return jnp.einsum(form, left.astype(jnp.float32), right.astype(jnp.float32))

def range_compress(spectra, reference):
    real_in = spectra[0].astype(jnp.float32)
    imag_in = spectra[1].astype(jnp.float32)
    matched = jnp.stack([real_in * reference[0] + imag_in * reference[1], imag_in * reference[0] - real_in * reference[1]]).astype(jnp.bfloat16)
    count = spectra.shape[1]
    outer_len = RSPLIT
    inner_len = RNG // RSPLIT
    shaped = matched.reshape(2, count, outer_len, inner_len)
    section = fdot('cnek,epkb->cpnb', dft_block(outer_len, 1), shaped)
    twc, tws = twiddle(outer_len, inner_len, RNG)
    first = jnp.stack([section[0] * twc - section[1] * tws, section[0] * tws + section[1] * twc]).astype(jnp.bfloat16)
    second = fdot('cmek,epnk->cpmn', dft_block(inner_len, 1), first)
    return second.reshape(2, count, RNG).astype(jnp.bfloat16)

def azimuth_focus(columns, reference):
    count = columns.shape[1]
    doppler = fdot('cuep,epk->cuk', dft_block(count, -1), columns)
    ref_re = reference[0].astype(jnp.float32)
    ref_im = reference[1].astype(jnp.float32)
    shaped = jnp.stack([doppler[0] * ref_re - doppler[1] * ref_im, doppler[0] * ref_im + doppler[1] * ref_re]).astype(jnp.bfloat16)
    return fdot('cuep,epk->cuk', dft_block(count, 1), shaped).astype(jnp.bfloat16)

def cross(first, second):
    fre = first[:, 0].astype(jnp.float32)
    fim = first[:, 1].astype(jnp.float32)
    sre = second[:, 0].astype(jnp.float32)
    sim = second[:, 1].astype(jnp.float32)
    return jnp.stack([fre * sre + fim * sim, fim * sre - fre * sim], axis=1)

def goldstein(patches):
    forward = dft_block(BLK, -1)
    backward = dft_block(BLK, 1)
    rows = fdot('cuei,npeij->npcuj', forward, patches).astype(jnp.bfloat16)
    spectrum = fdot('npeuj,cvej->npcuv', rows, forward)
    power = spectrum[:, :, 0] ** 2 + spectrum[:, :, 1] ** 2
    smooth = jnp.zeros_like(power)
    for down in (-1, 0, 1):
        for across in (-1, 0, 1):
            smooth = smooth + jnp.roll(power, (down, across), axis=(-2, -1))
    smooth = smooth / 9.0
    level = lax.optimization_barrier(jnp.mean(smooth, axis=(-2, -1), keepdims=True))
    weight = jnp.sqrt(jnp.sqrt(smooth / (level + 1e-06)))
    weighted = (spectrum * weight[:, :, None]).astype(jnp.bfloat16)
    back = fdot('cuei,npeij->npcuj', backward, weighted).astype(jnp.bfloat16)
    return fdot('npeuj,cvej->npcuv', back, backward).astype(jnp.bfloat16)

def date_tiles(spectra, range_reference, azimuth_reference, owners, slots, kinds):
    compressed = range_compress(spectra, range_reference)
    image = azimuth_focus(compressed, azimuth_reference)
    row_blocks = PULSES // BLK
    col_blocks = RNG // (N_SHARD * BLK)
    blocks = image.reshape(2, row_blocks, BLK, N_SHARD, col_blocks, BLK)
    blocks = jnp.transpose(blocks, (3, 1, 4, 0, 2, 5)).reshape(BLOCKS, 2, BLK, BLK)
    kernels = kernel_table()[kinds]
    resampled = fdot('nij,ncjk->ncik', kernels, blocks).astype(jnp.bfloat16)
    tiles = jnp.zeros((TILES, 2, BLK, BLK), jnp.bfloat16)
    return tiles.at[owners * CAP + slots].set(resampled)

def reference(echo_spectra, range_reference, azimuth_reference, block_owner, block_slot, kernel_index):
    mapped = [date_tiles(echo_spectra[d], range_reference, azimuth_reference, block_owner[d], block_slot[d], kernel_index[d]) for d in range(DATES)]
    results = []
    for d in range(DATES):
        pairs = jnp.stack([cross(mapped[d], mapped[(d + 1) % DATES]), cross(mapped[d], mapped[(d + 2) % DATES])], axis=1).astype(jnp.bfloat16)
        grouped = pairs.reshape(N_SHARD, CAP, 2, 2, BLK, BLK)
        done = lax.map(goldstein, grouped)
        results.append(done.reshape(TILES, 2, 2, BLK, BLK))
    return jnp.stack(results)
```

```python
import functools
import math

import jax
import jax.numpy as jnp
import ml_dtypes
import numpy as np
from jax import lax
from jax.experimental import pallas as pl
from jax.experimental.pallas import tpu as pltpu
from jax.sharding import PartitionSpec as P

BLK = 128
NSUB = 8
BLK_DEV = 8
BF = jnp.bfloat16
F32 = jnp.float32


def dft_parts(size, sign):
    index = np.arange(size)
    angle = 2.0 * math.pi / size * (index[:, None] * index[None, :] % size)
    scale = 1.0 / math.sqrt(size)
    return np.cos(angle) * scale, sign * np.sin(angle) * scale


def left_table(size, sign):
    cosine, sine = dft_parts(size, sign)
    return np.block([[cosine, -sine], [sine, cosine]]).astype(ml_dtypes.bfloat16)


def right_table(size, sign):
    return np.ascontiguousarray(left_table(size, sign).T)


def first_table(rng):
    outer, inner = BLK, rng // BLK
    low = outer * BLK // rng
    cosine, sine = dft_parts(outer, 1)
    full = np.stack([np.stack([cosine, sine], 1), np.stack([-sine, cosine], 1)])
    full = full.reshape(2, outer // low, low, 2 * outer)
    return np.transpose(full, (2, 0, 1, 3)).reshape(2 * outer, 2 * outer).astype(ml_dtypes.bfloat16)


def twiddle_table(rng):
    inner = rng // BLK
    phase = np.arange(inner)[:, None] * np.arange(BLK)[None, :] % rng
    angle = 2.0 * math.pi / rng * phase
    return np.stack([np.cos(angle), np.sin(angle)]).astype(np.float32)


def kernel_table():
    offset = (np.arange(NSUB) + 0.5) / NSUB
    cells = np.arange(BLK)
    dist = cells[None, None, :] - cells[None, :, None] - offset[:, None, None]
    window = np.where(np.abs(dist) < 4.0, 0.5 + 0.5 * np.cos(math.pi * dist / 4.0), 0.0)
    return (np.sinc(dist) * window).astype(ml_dtypes.bfloat16)


def mm(left, right):
    return jnp.dot(left, right, preferred_element_type=F32)


def kernel(
    n,
    dates,
    most,
    capacity,
    src_ref,
    kind_ref,
    entry_ref,
    valid_ref,
    echo_ref,
    rref_ref,
    aref_ref,
    t1_ref,
    tw_ref,
    w2_ref,
    pf_ref,
    pb_ref,
    kt_ref,
    gfl_ref,
    gfr_ref,
    gbl_ref,
    gbr_ref,
    out_ref,
    lhs,
    mat,
    snd,
    cols,
    blocks,
    outbox,
    inbox,
    ybox,
    xbox,
    fil,
    s1,
    r1,
    s2,
    r2,
    sy,
    ry,
    sx,
    rx,
):
    me = lax.axis_index("shard")
    day = lax.axis_index("date")
    grp = lax.axis_index("grp")
    relay = dates == 4
    ydst = lax.rem(day + dates - 2, dates)
    if relay:
        parity = lax.rem(day, 2)
        xdst = day + 1 - 2 * parity
        xsrc = xdst
    else:
        xdst = lax.rem(day + dates - 1, dates)
        xsrc = lax.rem(day + 1, dates)
    ysrc = lax.rem(day + 2, dates)
    mesh_id = pl.DeviceIdType.MESH

    barrier = pltpu.get_barrier_semaphore()

    def greet(k, _):
        pl.semaphore_signal(
            barrier, inc=1, device_id=(grp, day, lax.rem(me + k, n)), device_id_type=mesh_id
        )
        return 0

    lax.fori_loop(1, n, greet, 0)
    for other in (ysrc, xsrc):
        pl.semaphore_signal(barrier, inc=1, device_id=(grp, other, me), device_id_type=mesh_id)

    pulses = echo_ref.shape[1]
    rng = echo_ref.shape[2]
    tiles = rng // BLK
    inner = rng // BLK
    mine = tiles // n
    wide = n * pulses

    real = echo_ref[0].astype(F32)
    imag = echo_ref[1].astype(F32)
    rre = rref_ref[0:1, :]
    rim = rref_ref[1:2, :]
    mat[0] = (real * rre + imag * rim).reshape(pulses, tiles, BLK)
    mat[1] = (imag * rre - real * rim).reshape(pulses, tiles, BLK)

    for p in range(pulses):
        both = jnp.concatenate([mat[0, p], mat[1, p]], axis=0).T
        low = BLK // inner
        parts = [both[x * inner : (x + 1) * inner] for x in range(low)]
        lhs[p * inner : (p + 1) * inner, :] = jnp.concatenate(parts, axis=1).astype(BF)

    twc = tw_ref[0]
    tws = tw_ref[1]
    group = 4
    for g in range(0, pulses, group):
        section = mm(lhs[g * inner : (g + group) * inner, :], t1_ref[...])
        rights = []
        for p in range(group):
            sre = section[p * inner : (p + 1) * inner, :BLK]
            sim = section[p * inner : (p + 1) * inner, BLK:]
            rights.append(
                jnp.concatenate([sre * twc - sim * tws, sre * tws + sim * twc], axis=0).astype(BF)
            )
        second = mm(w2_ref[...], jnp.concatenate(rights, axis=1))
        for p in range(group):
            mat[:, g + p] = second[:, p * BLK : (p + 1) * BLK].reshape(2, tiles, BLK)
    for c in range(2):
        snd[c] = jnp.swapaxes(mat[c], 0, 1).astype(BF)

    pl.semaphore_wait(barrier, n + 1)

    def copy_one(k):
        dest = lax.rem(me + k, n)
        return pltpu.make_async_remote_copy(
            src_ref=snd.at[:, pl.ds(dest * mine, mine)],
            dst_ref=cols.at[:, :, pl.ds(me * pulses, pulses)],
            send_sem=s1.at[k],
            recv_sem=r1.at[k],
            device_id=(grp, day, dest),
            device_id_type=mesh_id,
        )

    def wait_one(k):
        source = lax.rem(me + n - k, n)
        return pltpu.make_async_remote_copy(
            src_ref=snd.at[:, pl.ds(me * mine, mine)],
            dst_ref=cols.at[:, :, pl.ds(source * pulses, pulses)],
            send_sem=s1.at[k],
            recv_sem=r1.at[k],
            device_id=(grp, day, source),
            device_id_type=mesh_id,
        )

    def start_one(k, _):
        copy_one(k).start()
        return 0

    def end_one(k, _):
        wait_one(k).wait_recv()
        return 0

    lax.fori_loop(1, n, start_one, 0)
    cols[:, :, pl.ds(me * pulses, pulses)] = snd[:, pl.ds(me * mine, mine)]
    lax.fori_loop(1, n, end_one, 0)

    rows_of = wide // BLK
    for j in range(0, mine, 2):
        right = jnp.concatenate(
            [
                jnp.concatenate([cols[0, j], cols[1, j]], axis=0),
                jnp.concatenate([cols[0, j + 1], cols[1, j + 1]], axis=0),
            ],
            axis=1,
        )
        doppler = mm(pf_ref[...], right)
        are = aref_ref[0, :, j * BLK : (j + 2) * BLK].astype(F32)
        aim = aref_ref[1, :, j * BLK : (j + 2) * BLK].astype(F32)
        dre = doppler[:wide]
        dim = doppler[wide:]
        shaped = jnp.concatenate([dre * are - dim * aim, dre * aim + dim * are], axis=0).astype(BF)
        image = mm(pb_ref[...], shaped).astype(BF)
        for x in range(2):
            for y in range(rows_of):
                for c in range(2):
                    low = c * wide + y * BLK
                    blocks[y * mine + j + x, :, c * BLK : (c + 1) * BLK] = image[
                        low : low + BLK, x * BLK : (x + 1) * BLK
                    ]

    def resampled(k, r):
        at = k * most + r
        return mm(kt_ref[kind_ref[at]], blocks[src_ref[at]]).astype(BF)

    for r in range(most):
        inbox[0, r] = resampled(0, r)

    def copy_two(k, dest):
        return pltpu.make_async_remote_copy(
            src_ref=outbox.at[k],
            dst_ref=inbox.at[k],
            send_sem=s2.at[k],
            recv_sem=r2.at[k],
            device_id=(grp, day, dest),
            device_id_type=mesh_id,
        )

    def start_two(k, _):
        for r in range(most):
            outbox[k, r] = resampled(k, r)
        copy_two(k, lax.rem(me + k, n)).start()
        return 0

    lax.fori_loop(1, n, start_two, 0)

    def copy_y(k):
        return pltpu.make_async_remote_copy(
            src_ref=inbox.at[k],
            dst_ref=ybox.at[k],
            send_sem=sy.at[k],
            recv_sem=ry.at[k],
            device_id=(grp, ydst, me),
            device_id_type=mesh_id,
        )

    def copy_x(k, source):
        return pltpu.make_async_remote_copy(
            src_ref=source.at[k],
            dst_ref=xbox.at[k],
            send_sem=sx.at[k],
            recv_sem=rx.at[k],
            device_id=(grp, xdst, me),
            device_id_type=mesh_id,
        )

    def stage_a(k):
        @pl.when(k > 0)
        def _():
            copy_two(k, lax.rem(me + k, n)).wait_recv()

        copy_y(k).start()
        if relay:

            @pl.when(parity == 1)
            def _():
                copy_x(k, inbox).start()
        else:
            copy_x(k, inbox).start()

    def stage_b(k):
        copy_y(k).wait_recv()
        if relay:

            @pl.when(parity == 0)
            def _():
                copy_x(k, ybox).start()

    def patches(k, r):
        own = inbox[k, r].astype(F32)
        ore = own[:, :BLK]
        oim = own[:, BLK:]
        tops = []
        lows = []
        for box in (xbox, ybox):
            oth = box[k, r].astype(F32)
            tre = oth[:, :BLK]
            tim = oth[:, BLK:]
            tops.append(ore * tre + oim * tim)
            lows.append(oim * tre - ore * tim)
        pair = jnp.concatenate(
            [jnp.concatenate(tops, axis=1), jnp.concatenate(lows, axis=1)], axis=0
        ).astype(BF)

        def turned(x):
            return jnp.concatenate(
                [
                    jnp.concatenate([x[:BLK, :BLK], x[BLK:, :BLK]], axis=1),
                    jnp.concatenate([x[:BLK, BLK:], x[BLK:, BLK:]], axis=1),
                ],
                axis=0,
            )

        rows = mm(gfl_ref[...], pair).astype(BF)
        spectrum = mm(turned(rows), gfr_ref[...])
        weighted = []
        for x in range(2):
            spec = spectrum[x * BLK : (x + 1) * BLK]
            sre = spec[:, :BLK]
            sim = spec[:, BLK:]
            power = sre * sre + sim * sim
            line = power + pltpu.roll(power, 1, 1) + pltpu.roll(power, BLK - 1, 1)
            smooth = (line + pltpu.roll(line, 1, 0) + pltpu.roll(line, BLK - 1, 0)) * (1.0 / 9.0)
            level = jnp.sum(jnp.sum(smooth, axis=0, keepdims=True), axis=1, keepdims=True)
            level = level * (1.0 / (BLK * BLK)) + 1e-06
            weight = lax.rsqrt(lax.rsqrt(smooth * (1.0 / level)))
            weighted.append(jnp.concatenate([sre * weight, sim * weight], axis=1))
        weighted = jnp.concatenate(weighted, axis=0).astype(BF)
        back = mm(gbl_ref[...], turned(weighted)).astype(BF)
        done = mm(turned(back), gbr_ref[...]).astype(BF)
        at = k * most + r
        for x in range(2):
            for c in range(2):
                fil[at, x, c] = done[x * BLK : (x + 1) * BLK, c * BLK : (c + 1) * BLK]

    def stage_c(k):
        copy_x(k, inbox).wait_recv()
        for r in range(most):
            patches(k, r)

    stage_a(0)
    stage_a(1)
    stage_b(0)

    def step(k, _):
        stage_a(k)
        stage_b(k - 1)
        stage_c(k - 2)
        return 0

    lax.fori_loop(2, n, step, 0)
    stage_b(n - 1)

    def last(k, _):
        stage_c(k)
        return 0

    lax.fori_loop(n - 2, n, last, 0)

    def place(q, _):
        found = fil[entry_ref[q]]
        out_ref[q] = jnp.where(valid_ref[q] == 1, found, jnp.zeros_like(found))
        return 0

    lax.fori_loop(0, capacity, place, 0)

    def drain(k, _):
        @pl.when(k > 0)
        def _():
            copy_one(k).wait_send()
            copy_two(k, lax.rem(me + k, n)).wait_send()

        copy_y(k).wait_send()
        copy_x(k, inbox).wait_send()
        return 0

    lax.fori_loop(0, n, drain, 0)


def body(dates, echo_spectra, range_reference, azimuth_reference, block_owner, block_slot, kernel_index):
    n = lax.axis_size("shard")
    most = max(2, 2 * BLK_DEV // n)
    capacity = min(2 * BLK_DEV, n * most)
    me = lax.axis_index("shard")
    owners = block_owner[0].reshape(n, BLK_DEV)
    slots = block_slot[0]
    local = jnp.arange(BLK_DEV, dtype=jnp.int32)
    earlier = (owners[:, :, None] == owners[:, None, :]) & (local[None, None, :] < local[None, :, None])
    rank = jnp.sum(earlier.astype(jnp.int32), axis=2)
    steps = jnp.arange(n, dtype=jnp.int32)
    my_owner = lax.dynamic_index_in_dim(owners, me, 0, keepdims=False)
    my_rank = lax.dynamic_index_in_dim(rank, me, 0, keepdims=False)
    my_kind = lax.dynamic_index_in_dim(kernel_index[0].reshape(n, BLK_DEV), me, 0, keepdims=False)
    my_place = (my_owner - me + n) % n * most + my_rank
    match = (my_place[None, :] == jnp.arange(n * most, dtype=jnp.int32)[:, None]).astype(jnp.int32)
    source = jnp.sum(match * local[None, :], axis=1)
    kind = jnp.sum(match * my_kind[None, :], axis=1)
    entry_of = ((me - steps + n) % n * most)[:, None] + rank
    hit = (slots[None, :] == jnp.arange(capacity, dtype=jnp.int32)[:, None]) & (
        owners.reshape(-1) == me
    )[None, :]
    entry = jnp.sum(hit.astype(jnp.int32) * entry_of.reshape(-1)[None, :], axis=1)
    valid = jnp.max(hit.astype(jnp.int32), axis=1)

    echo = echo_spectra[0]
    pulses, rng = echo.shape[1:]
    inner = rng // BLK
    mine = rng // BLK // n
    wide = pulses * n
    tables = [
        first_table(rng),
        twiddle_table(rng),
        left_table(inner, 1),
        left_table(wide, -1),
        left_table(wide, 1),
        kernel_table(),
        left_table(BLK, -1),
        right_table(BLK, -1),
        left_table(BLK, 1),
        right_table(BLK, 1),
    ]
    smem = pl.BlockSpec(memory_space=pltpu.SMEM)
    vmem = pl.BlockSpec(memory_space=pltpu.VMEM)
    box = pltpu.VMEM((n, most, BLK, 2 * BLK), BF)
    sems = pltpu.SemaphoreType.DMA((n,))
    out = pl.pallas_call(
        functools.partial(kernel, n, dates, most, capacity),
        out_shape=jax.ShapeDtypeStruct((capacity, 2, 2, BLK, BLK), BF),
        in_specs=[smem] * 4 + [vmem] * 13,
        out_specs=vmem,
        scratch_shapes=[
            pltpu.VMEM((pulses * inner, 2 * BLK), BF),
            pltpu.VMEM((2, pulses, rng // BLK, BLK), F32),
            pltpu.VMEM((2, rng // BLK, pulses, BLK), BF),
            pltpu.VMEM((2, mine, wide, BLK), BF),
            pltpu.VMEM((BLK_DEV, BLK, 2 * BLK), BF),
            box,
            box,
            box,
            box,
            pltpu.VMEM((n * most, 2, 2, BLK, BLK), BF),
            *[sems] * 8,
        ],
        compiler_params=pltpu.CompilerParams(collective_id=0, has_side_effects=True),
    )(source, kind, entry, valid, echo, range_reference, azimuth_reference, *[jnp.asarray(t) for t in tables])
    return out[None]


def solution(mesh):
    in_specs = (
        P(("grp", "date"), None, "shard", None),
        P(),
        P(None, None, "shard"),
        P(("grp", "date"), None),
        P(("grp", "date"), None),
        P(("grp", "date"), None),
    )
    out_specs = P(("grp", "date"), "shard", None, None, None, None)
    return jax.shard_map(
        functools.partial(body, mesh.shape["date"]),
        mesh=mesh,
        in_specs=in_specs,
        out_specs=out_specs,
        check_vma=False,
    )
```

```python
import functools
import math

import jax
import jax.numpy as jnp
import ml_dtypes
import numpy as np
from jax import lax
from jax.experimental import pallas as pl
from jax.experimental.pallas import tpu as pltpu
from jax.sharding import PartitionSpec as P

BLK = 128
NSUB = 8
BLK_DEV = 8
BF = jnp.bfloat16
F32 = jnp.float32


def dft_parts(size, sign):
    index = np.arange(size)
    angle = 2.0 * math.pi / size * (index[:, None] * index[None, :] % size)
    scale = 1.0 / math.sqrt(size)
    return np.cos(angle) * scale, sign * np.sin(angle) * scale


def left_table(size, sign):
    cosine, sine = dft_parts(size, sign)
    return np.block([[cosine, -sine], [sine, cosine]]).astype(ml_dtypes.bfloat16)


def right_table(size, sign):
    return np.ascontiguousarray(left_table(size, sign).T)


def first_table(rng):
    outer, inner = BLK, rng // BLK
    low = outer * BLK // rng
    cosine, sine = dft_parts(outer, 1)
    full = np.stack([np.stack([cosine, sine], 1), np.stack([-sine, cosine], 1)])
    full = full.reshape(2, outer // low, low, 2 * outer)
    return np.transpose(full, (2, 0, 1, 3)).reshape(2 * outer, 2 * outer).astype(ml_dtypes.bfloat16)


def twiddle_table(rng):
    inner = rng // BLK
    phase = np.arange(inner)[:, None] * np.arange(BLK)[None, :] % rng
    angle = 2.0 * math.pi / rng * phase
    return np.stack([np.cos(angle), np.sin(angle)]).astype(np.float32)


def kernel_table():
    offset = (np.arange(NSUB) + 0.5) / NSUB
    cells = np.arange(BLK)
    dist = cells[None, None, :] - cells[None, :, None] - offset[:, None, None]
    window = np.where(np.abs(dist) < 4.0, 0.5 + 0.5 * np.cos(math.pi * dist / 4.0), 0.0)
    return (np.sinc(dist) * window).astype(ml_dtypes.bfloat16)


def mm(left, right):
    return jnp.dot(left, right, preferred_element_type=F32)


def kernel(
    n,
    dates,
    most,
    capacity,
    owner_ref,
    slot_ref,
    kinds_ref,
    echo_ref,
    rref_ref,
    aref_ref,
    t1_ref,
    tw_ref,
    w2_ref,
    pf_ref,
    pb_ref,
    kt_ref,
    gfl_ref,
    gfr_ref,
    gbl_ref,
    gbr_ref,
    fil,
    entry_ref,
    src_ref,
    kind_ref,
    lhs,
    mat,
    snd,
    cols,
    blocks,
    outbox,
    inbox,
    ybox,
    xbox,
    s1,
    r1,
    s2,
    r2,
    sy,
    ry,
    sx,
    rx,
):
    me = lax.axis_index("shard")
    day = lax.axis_index("date")
    grp = lax.axis_index("grp")
    relay = dates == 4
    ydst = lax.rem(day + dates - 2, dates)
    if relay:
        parity = lax.rem(day, 2)
        xdst = day + 1 - 2 * parity
        xsrc = xdst
    else:
        xdst = lax.rem(day + dates - 1, dates)
        xsrc = lax.rem(day + 1, dates)
    ysrc = lax.rem(day + 2, dates)
    mesh_id = pl.DeviceIdType.MESH

    barrier = pltpu.get_barrier_semaphore()

    def greet(k, _):
        pl.semaphore_signal(
            barrier, inc=1, device_id=(grp, day, lax.rem(me + k, n)), device_id_type=mesh_id
        )
        return 0

    lax.fori_loop(1, n, greet, 0)
    for other in (ysrc, xsrc):
        pl.semaphore_signal(barrier, inc=1, device_id=(grp, other, me), device_id_type=mesh_id)

    pulses = echo_ref.shape[1]
    rng = echo_ref.shape[2]
    tiles = rng // BLK
    inner = rng // BLK
    mine = tiles // n
    wide = n * pulses

    real = echo_ref[0].astype(F32)
    imag = echo_ref[1].astype(F32)
    rre = rref_ref[0:1, :]
    rim = rref_ref[1:2, :]
    mat[0] = (real * rre + imag * rim).reshape(pulses, tiles, BLK)
    mat[1] = (imag * rre - real * rim).reshape(pulses, tiles, BLK)

    for p in range(pulses):
        both = jnp.concatenate([mat[0, p], mat[1, p]], axis=0).T
        low = BLK // inner
        parts = [both[x * inner : (x + 1) * inner] for x in range(low)]
        lhs[p * inner : (p + 1) * inner, :] = jnp.concatenate(parts, axis=1).astype(BF)

    twc = tw_ref[0]
    tws = tw_ref[1]
    group = 4
    for g in range(0, pulses, group):
        section = mm(lhs[g * inner : (g + group) * inner, :], t1_ref[...])
        rights = []
        for p in range(group):
            sre = section[p * inner : (p + 1) * inner, :BLK]
            sim = section[p * inner : (p + 1) * inner, BLK:]
            rights.append(
                jnp.concatenate([sre * twc - sim * tws, sre * tws + sim * twc], axis=0).astype(BF)
            )
        second = mm(w2_ref[...], jnp.concatenate(rights, axis=1))
        for p in range(group):
            mat[:, g + p] = second[:, p * BLK : (p + 1) * BLK].reshape(2, tiles, BLK)
    for c in range(2):
        snd[c] = jnp.swapaxes(mat[c], 0, 1).astype(BF)

    pl.semaphore_wait(barrier, n + 1)

    def copy_one(k):
        dest = lax.rem(me + k, n)
        return pltpu.make_async_remote_copy(
            src_ref=snd.at[:, pl.ds(dest * mine, mine)],
            dst_ref=cols.at[:, :, pl.ds(me * pulses, pulses)],
            send_sem=s1.at[k],
            recv_sem=r1.at[k],
            device_id=(grp, day, dest),
            device_id_type=mesh_id,
        )

    def wait_one(k):
        source = lax.rem(me + n - k, n)
        return pltpu.make_async_remote_copy(
            src_ref=snd.at[:, pl.ds(me * mine, mine)],
            dst_ref=cols.at[:, :, pl.ds(source * pulses, pulses)],
            send_sem=s1.at[k],
            recv_sem=r1.at[k],
            device_id=(grp, day, source),
            device_id_type=mesh_id,
        )

    def start_one(k, _):
        copy_one(k).start()
        return 0

    def end_one(k, _):
        wait_one(k).wait_recv()
        return 0

    lax.fori_loop(1, n, start_one, 0)
    cols[:, :, pl.ds(me * pulses, pulses)] = snd[:, pl.ds(me * mine, mine)]

    def sources(k, _):
        dest = lax.rem(me + k, n)
        seen = jnp.int32(0)
        found = [jnp.int32(0)] * most
        for b in range(BLK_DEV):
            named = owner_ref[0, me * BLK_DEV + b] == dest
            for r in range(most):
                found[r] = jnp.where(named & (seen == r), b, found[r])
            seen = seen + named.astype(jnp.int32)
        for r in range(most):
            src_ref[k * most + r] = found[r]
            kind_ref[k * most + r] = kinds_ref[0, me * BLK_DEV + found[r]]
        return 0

    lax.fori_loop(0, n, sources, 0)

    def entries(t, held):
        held = list(held)
        at = lax.rem(me - t + n, n) * most
        for b in range(BLK_DEV):
            named = owner_ref[0, t * BLK_DEV + b] == me
            slot = jnp.where(named, slot_ref[0, t * BLK_DEV + b], -1)
            for q in range(capacity):
                held[q] = jnp.where(slot == q, at, held[q])
            at = at + named.astype(jnp.int32)
        return tuple(held)

    held = lax.fori_loop(0, n, entries, (jnp.int32(n * most),) * capacity)
    for q in range(capacity):
        entry_ref[q] = held[q]
    fil[n * most] = jnp.zeros_like(fil[n * most])
    lax.fori_loop(1, n, end_one, 0)

    rows_of = wide // BLK
    for j in range(0, mine, 2):
        right = jnp.concatenate(
            [
                jnp.concatenate([cols[0, j], cols[1, j]], axis=0),
                jnp.concatenate([cols[0, j + 1], cols[1, j + 1]], axis=0),
            ],
            axis=1,
        )
        doppler = mm(pf_ref[...], right)
        are = aref_ref[0, :, j * BLK : (j + 2) * BLK].astype(F32)
        aim = aref_ref[1, :, j * BLK : (j + 2) * BLK].astype(F32)
        dre = doppler[:wide]
        dim = doppler[wide:]
        shaped = jnp.concatenate([dre * are - dim * aim, dre * aim + dim * are], axis=0).astype(BF)
        image = mm(pb_ref[...], shaped).astype(BF)
        for x in range(2):
            for y in range(rows_of):
                for c in range(2):
                    low = c * wide + y * BLK
                    blocks[y * mine + j + x, :, c * BLK : (c + 1) * BLK] = image[
                        low : low + BLK, x * BLK : (x + 1) * BLK
                    ]

    def resampled(k, r):
        at = k * most + r
        return mm(kt_ref[kind_ref[at]], blocks[src_ref[at]]).astype(BF)

    for r in range(most):
        inbox[0, r] = resampled(0, r)

    def copy_two(k, dest):
        return pltpu.make_async_remote_copy(
            src_ref=outbox.at[k],
            dst_ref=inbox.at[k],
            send_sem=s2.at[k],
            recv_sem=r2.at[k],
            device_id=(grp, day, dest),
            device_id_type=mesh_id,
        )

    def start_two(k, _):
        for r in range(most):
            outbox[k, r] = resampled(k, r)
        copy_two(k, lax.rem(me + k, n)).start()
        return 0

    lax.fori_loop(1, n, start_two, 0)

    def copy_y(k):
        return pltpu.make_async_remote_copy(
            src_ref=inbox.at[k],
            dst_ref=ybox.at[k],
            send_sem=sy.at[k],
            recv_sem=ry.at[k],
            device_id=(grp, ydst, me),
            device_id_type=mesh_id,
        )

    def copy_x(k, source):
        return pltpu.make_async_remote_copy(
            src_ref=source.at[k],
            dst_ref=xbox.at[k],
            send_sem=sx.at[k],
            recv_sem=rx.at[k],
            device_id=(grp, xdst, me),
            device_id_type=mesh_id,
        )

    def stage_a(k):
        @pl.when(k > 0)
        def _():
            copy_two(k, lax.rem(me + k, n)).wait_recv()

        copy_y(k).start()
        if relay:

            @pl.when(parity == 1)
            def _():
                copy_x(k, inbox).start()
        else:
            copy_x(k, inbox).start()

    def stage_b(k):
        copy_y(k).wait_recv()
        if relay:

            @pl.when(parity == 0)
            def _():
                copy_x(k, ybox).start()

    def patches(k, r):
        own = inbox[k, r].astype(F32)
        ore = own[:, :BLK]
        oim = own[:, BLK:]
        tops = []
        lows = []
        for box in (xbox, ybox):
            oth = box[k, r].astype(F32)
            tre = oth[:, :BLK]
            tim = oth[:, BLK:]
            tops.append(ore * tre + oim * tim)
            lows.append(oim * tre - ore * tim)
        pair = jnp.concatenate(
            [jnp.concatenate(tops, axis=1), jnp.concatenate(lows, axis=1)], axis=0
        ).astype(BF)

        def turned(x):
            return jnp.concatenate(
                [
                    jnp.concatenate([x[:BLK, :BLK], x[BLK:, :BLK]], axis=1),
                    jnp.concatenate([x[:BLK, BLK:], x[BLK:, BLK:]], axis=1),
                ],
                axis=0,
            )

        rows = mm(gfl_ref[...], pair).astype(BF)
        spectrum = mm(turned(rows), gfr_ref[...])
        weighted = []
        for x in range(2):
            spec = spectrum[x * BLK : (x + 1) * BLK]
            sre = spec[:, :BLK]
            sim = spec[:, BLK:]
            power = sre * sre + sim * sim
            line = power + pltpu.roll(power, 1, 1) + pltpu.roll(power, BLK - 1, 1)
            smooth = (line + pltpu.roll(line, 1, 0) + pltpu.roll(line, BLK - 1, 0)) * (1.0 / 9.0)
            level = jnp.sum(jnp.sum(smooth, axis=0, keepdims=True), axis=1, keepdims=True)
            level = level * (1.0 / (BLK * BLK)) + 1e-06
            weight = lax.rsqrt(lax.rsqrt(smooth * (1.0 / level)))
            weighted.append(jnp.concatenate([sre * weight, sim * weight], axis=1))
        weighted = jnp.concatenate(weighted, axis=0).astype(BF)
        back = mm(gbl_ref[...], turned(weighted)).astype(BF)
        done = mm(turned(back), gbr_ref[...]).astype(BF)
        at = k * most + r
        for x in range(2):
            for c in range(2):
                fil[at, x, c] = done[x * BLK : (x + 1) * BLK, c * BLK : (c + 1) * BLK]

    def stage_c(k):
        copy_x(k, inbox).wait_recv()
        for r in range(most):
            patches(k, r)

    stage_a(0)
    stage_a(1)
    stage_b(0)

    def step(k, _):
        stage_a(k)
        stage_b(k - 1)
        stage_c(k - 2)
        return 0

    lax.fori_loop(2, n, step, 0)
    stage_b(n - 1)

    def last(k, _):
        stage_c(k)
        return 0

    lax.fori_loop(n - 2, n, last, 0)

    def drain(k, _):
        @pl.when(k > 0)
        def _():
            copy_one(k).wait_send()
            copy_two(k, lax.rem(me + k, n)).wait_send()

        copy_y(k).wait_send()
        copy_x(k, inbox).wait_send()
        return 0

    lax.fori_loop(0, n, drain, 0)


def place(capacity, entry_ref, fil, out_ref, sems):
    def copy(q):
        return pltpu.make_async_copy(fil.at[entry_ref[q]], out_ref.at[q], sems.at[q])

    for q in range(capacity):
        copy(q).start()
    for q in range(capacity):
        copy(q).wait()


def body(dates, echo_spectra, range_reference, azimuth_reference, block_owner, block_slot, kernel_index):
    n = lax.axis_size("shard")
    most = max(2, 2 * BLK_DEV // n)
    capacity = min(2 * BLK_DEV, n * most)
    echo = echo_spectra[0]
    pulses, rng = echo.shape[1:]
    inner = rng // BLK
    mine = rng // BLK // n
    wide = pulses * n
    tables = [
        first_table(rng),
        twiddle_table(rng),
        left_table(inner, 1),
        left_table(wide, -1),
        left_table(wide, 1),
        kernel_table(),
        left_table(BLK, -1),
        right_table(BLK, -1),
        left_table(BLK, 1),
        right_table(BLK, 1),
    ]
    smem = pl.BlockSpec(memory_space=pltpu.SMEM)
    vmem = pl.BlockSpec(memory_space=pltpu.VMEM)
    box = pltpu.VMEM((n, most, BLK, 2 * BLK), BF)
    sems = pltpu.SemaphoreType.DMA((n,))
    filtered, entry = pl.pallas_call(
        functools.partial(kernel, n, dates, most, capacity),
        out_shape=(
            jax.ShapeDtypeStruct((n * most + 1, 2, 2, BLK, BLK), BF),
            jax.ShapeDtypeStruct((capacity,), jnp.int32),
        ),
        in_specs=[smem] * 3 + [vmem] * 13,
        out_specs=(vmem, smem),
        scratch_shapes=[
            pltpu.SMEM((n * most,), jnp.int32),
            pltpu.SMEM((n * most,), jnp.int32),
            pltpu.VMEM((pulses * inner, 2 * BLK), BF),
            pltpu.VMEM((2, pulses, rng // BLK, BLK), F32),
            pltpu.VMEM((2, rng // BLK, pulses, BLK), BF),
            pltpu.VMEM((2, mine, wide, BLK), BF),
            pltpu.VMEM((BLK_DEV, BLK, 2 * BLK), BF),
            box,
            box,
            box,
            box,
            *[sems] * 8,
        ],
        compiler_params=pltpu.CompilerParams(collective_id=0, has_side_effects=True),
    )(
        block_owner,
        block_slot,
        kernel_index,
        echo,
        range_reference,
        azimuth_reference,
        *[jnp.asarray(t) for t in tables],
    )
    out = pl.pallas_call(
        functools.partial(place, capacity),
        out_shape=jax.ShapeDtypeStruct((capacity, 2, 2, BLK, BLK), BF),
        in_specs=[smem, vmem],
        out_specs=pl.BlockSpec(memory_space=pl.ANY),
        scratch_shapes=[pltpu.SemaphoreType.DMA((capacity,))],
    )(entry, filtered)
    return out[None]


def solution(mesh):
    in_specs = (
        P(("grp", "date"), None, "shard", None),
        P(),
        P(None, None, "shard"),
        P(("grp", "date"), None),
        P(("grp", "date"), None),
        P(("grp", "date"), None),
    )
    out_specs = P(("grp", "date"), "shard", None, None, None, None)
    return jax.shard_map(
        functools.partial(body, mesh.shape["date"]),
        mesh=mesh,
        in_specs=in_specs,
        out_specs=out_specs,
        check_vma=False,
    )
```

```python
import functools
import math

import jax
import jax.numpy as jnp
import ml_dtypes
import numpy as np
from jax import lax
from jax.experimental import pallas as pl
from jax.experimental.pallas import tpu as pltpu
from jax.sharding import PartitionSpec as P

BLK = 128
NSUB = 8
BLK_DEV = 8
BF = jnp.bfloat16
F32 = jnp.float32


def dft_parts(size, sign):
    index = np.arange(size)
    angle = 2.0 * math.pi / size * (index[:, None] * index[None, :] % size)
    scale = 1.0 / math.sqrt(size)
    return np.cos(angle) * scale, sign * np.sin(angle) * scale


def left_table(size, sign):
    cosine, sine = dft_parts(size, sign)
    return np.block([[cosine, -sine], [sine, cosine]]).astype(ml_dtypes.bfloat16)


def right_table(size, sign):
    return np.ascontiguousarray(left_table(size, sign).T)


def first_table(rng):
    outer, inner = BLK, rng // BLK
    low = outer * BLK // rng
    cosine, sine = dft_parts(outer, 1)
    full = np.stack([np.stack([cosine, sine], 1), np.stack([-sine, cosine], 1)])
    full = full.reshape(2, outer // low, low, 2 * outer)
    return np.transpose(full, (2, 0, 1, 3)).reshape(2 * outer, 2 * outer).astype(ml_dtypes.bfloat16)


def twiddle_table(rng):
    inner = rng // BLK
    phase = np.arange(inner)[:, None] * np.arange(BLK)[None, :] % rng
    angle = 2.0 * math.pi / rng * phase
    return np.stack([np.cos(angle), np.sin(angle)]).astype(np.float32)


def kernel_table():
    offset = (np.arange(NSUB) + 0.5) / NSUB
    cells = np.arange(BLK)
    dist = cells[None, None, :] - cells[None, :, None] - offset[:, None, None]
    window = np.where(np.abs(dist) < 4.0, 0.5 + 0.5 * np.cos(math.pi * dist / 4.0), 0.0)
    return (np.sinc(dist) * window).astype(ml_dtypes.bfloat16)


def flipped(a, b, n):
    total = 0
    bit = 1
    while bit < n:
        total = total + (a // bit + b // bit) % 2 * bit
        bit *= 2
    return total


def mm(left, right):
    return jnp.dot(left, right, preferred_element_type=F32)


def kernel(
    n,
    dates,
    most,
    capacity,
    owner_ref,
    slot_ref,
    kinds_ref,
    echo_ref,
    rref_ref,
    aref_ref,
    t1_ref,
    tw_ref,
    w2_ref,
    pf_ref,
    pb_ref,
    kt_ref,
    gfl_ref,
    gfr_ref,
    gbl_ref,
    gbr_ref,
    fil,
    entry_ref,
    src_ref,
    kind_ref,
    lhs,
    mat,
    snd,
    cols,
    blocks,
    outbox,
    inbox,
    ybox,
    xbox,
    s1,
    r1,
    s2,
    r2,
    sy,
    ry,
    sx,
    rx,
):
    me = lax.axis_index("shard")
    day = lax.axis_index("date")
    grp = lax.axis_index("grp")
    relay = dates == 4
    ydst = lax.rem(day + dates - 2, dates)
    if relay:
        parity = lax.rem(day, 2)
        xdst = day + 1 - 2 * parity
        xsrc = xdst
    else:
        xdst = lax.rem(day + dates - 1, dates)
        xsrc = lax.rem(day + 1, dates)
    ysrc = lax.rem(day + 2, dates)
    mesh_id = pl.DeviceIdType.MESH

    barrier = pltpu.get_barrier_semaphore()

    def greet(k, _):
        pl.semaphore_signal(
            barrier, inc=1, device_id=(grp, day, flipped(me, k, n)), device_id_type=mesh_id
        )
        return 0

    lax.fori_loop(1, n, greet, 0)
    for other in (ysrc, xsrc):
        pl.semaphore_signal(barrier, inc=1, device_id=(grp, other, me), device_id_type=mesh_id)

    pulses = echo_ref.shape[1]
    rng = echo_ref.shape[2]
    tiles = rng // BLK
    inner = rng // BLK
    mine = tiles // n
    wide = n * pulses

    real = echo_ref[0].astype(F32)
    imag = echo_ref[1].astype(F32)
    rre = rref_ref[0:1, :]
    rim = rref_ref[1:2, :]
    mat[0] = (real * rre + imag * rim).reshape(pulses, tiles, BLK)
    mat[1] = (imag * rre - real * rim).reshape(pulses, tiles, BLK)

    for p in range(pulses):
        both = jnp.concatenate([mat[0, p], mat[1, p]], axis=0).T
        low = BLK // inner
        parts = [both[x * inner : (x + 1) * inner] for x in range(low)]
        lhs[p * inner : (p + 1) * inner, :] = jnp.concatenate(parts, axis=1).astype(BF)

    twc = tw_ref[0]
    tws = tw_ref[1]
    group = 4
    for g in range(0, pulses, group):
        section = mm(lhs[g * inner : (g + group) * inner, :], t1_ref[...])
        rights = []
        for p in range(group):
            sre = section[p * inner : (p + 1) * inner, :BLK]
            sim = section[p * inner : (p + 1) * inner, BLK:]
            rights.append(
                jnp.concatenate([sre * twc - sim * tws, sre * tws + sim * twc], axis=0).astype(BF)
            )
        second = mm(w2_ref[...], jnp.concatenate(rights, axis=1))
        for p in range(group):
            mat[:, g + p] = second[:, p * BLK : (p + 1) * BLK].reshape(2, tiles, BLK)
    for c in range(2):
        snd[c] = jnp.swapaxes(mat[c], 0, 1).astype(BF)

    pl.semaphore_wait(barrier, n + 1)

    def copy_one(k):
        dest = flipped(me, k, n)
        return pltpu.make_async_remote_copy(
            src_ref=snd.at[:, pl.ds(dest * mine, mine)],
            dst_ref=cols.at[:, :, pl.ds(me * pulses, pulses)],
            send_sem=s1.at[k],
            recv_sem=r1.at[k],
            device_id=(grp, day, dest),
            device_id_type=mesh_id,
        )

    def wait_one(k):
        source = flipped(me, k, n)
        return pltpu.make_async_remote_copy(
            src_ref=snd.at[:, pl.ds(me * mine, mine)],
            dst_ref=cols.at[:, :, pl.ds(source * pulses, pulses)],
            send_sem=s1.at[k],
            recv_sem=r1.at[k],
            device_id=(grp, day, source),
            device_id_type=mesh_id,
        )

    def start_one(k, _):
        copy_one(k).start()
        return 0

    def end_one(k, _):
        wait_one(k).wait_recv()
        return 0

    lax.fori_loop(1, n, start_one, 0)
    cols[:, :, pl.ds(me * pulses, pulses)] = snd[:, pl.ds(me * mine, mine)]

    def sources(k, _):
        dest = flipped(me, k, n)
        seen = jnp.int32(0)
        found = [jnp.int32(0)] * most
        for b in range(BLK_DEV):
            named = owner_ref[0, me * BLK_DEV + b] == dest
            for r in range(most):
                found[r] = jnp.where(named & (seen == r), b, found[r])
            seen = seen + named.astype(jnp.int32)
        for r in range(most):
            src_ref[k * most + r] = found[r]
            kind_ref[k * most + r] = kinds_ref[0, me * BLK_DEV + found[r]]
        return 0

    lax.fori_loop(0, n, sources, 0)

    def entries(t, held):
        held = list(held)
        at = flipped(me, t, n) * most
        for b in range(BLK_DEV):
            named = owner_ref[0, t * BLK_DEV + b] == me
            slot = jnp.where(named, slot_ref[0, t * BLK_DEV + b], -1)
            for q in range(capacity):
                held[q] = jnp.where(slot == q, at, held[q])
            at = at + named.astype(jnp.int32)
        return tuple(held)

    held = lax.fori_loop(0, n, entries, (jnp.int32(n * most),) * capacity)
    for q in range(capacity):
        entry_ref[q] = held[q]
    fil[n * most] = jnp.zeros_like(fil[n * most])
    lax.fori_loop(1, n, end_one, 0)

    rows_of = wide // BLK
    for j in range(0, mine, 2):
        right = jnp.concatenate(
            [
                jnp.concatenate([cols[0, j], cols[1, j]], axis=0),
                jnp.concatenate([cols[0, j + 1], cols[1, j + 1]], axis=0),
            ],
            axis=1,
        )
        doppler = mm(pf_ref[...], right)
        are = aref_ref[0, :, j * BLK : (j + 2) * BLK].astype(F32)
        aim = aref_ref[1, :, j * BLK : (j + 2) * BLK].astype(F32)
        dre = doppler[:wide]
        dim = doppler[wide:]
        shaped = jnp.concatenate([dre * are - dim * aim, dre * aim + dim * are], axis=0).astype(BF)
        image = mm(pb_ref[...], shaped).astype(BF)
        for x in range(2):
            for y in range(rows_of):
                for c in range(2):
                    low = c * wide + y * BLK
                    blocks[y * mine + j + x, :, c * BLK : (c + 1) * BLK] = image[
                        low : low + BLK, x * BLK : (x + 1) * BLK
                    ]

    def resampled(at):
        return mm(kt_ref[kind_ref[at]], blocks[src_ref[at]]).astype(BF)

    total = n * most
    for e in range(most):
        inbox[e] = resampled(e)

    def copy_two(e):
        return pltpu.make_async_remote_copy(
            src_ref=outbox.at[e],
            dst_ref=inbox.at[e],
            send_sem=s2.at[e],
            recv_sem=r2.at[e],
            device_id=(grp, day, flipped(me, e // most, n)),
            device_id_type=mesh_id,
        )

    def start_two(e, _):
        outbox[e] = resampled(e)
        copy_two(e).start()
        return 0

    lax.fori_loop(most, total, start_two, 0)

    def copy_y(k):
        return pltpu.make_async_remote_copy(
            src_ref=inbox.at[k],
            dst_ref=ybox.at[k],
            send_sem=sy.at[k],
            recv_sem=ry.at[k],
            device_id=(grp, ydst, me),
            device_id_type=mesh_id,
        )

    def copy_x(k, source):
        return pltpu.make_async_remote_copy(
            src_ref=source.at[k],
            dst_ref=xbox.at[k],
            send_sem=sx.at[k],
            recv_sem=rx.at[k],
            device_id=(grp, xdst, me),
            device_id_type=mesh_id,
        )

    def stage_a(k):
        if not isinstance(k, int) or k >= most:
            copy_two(k).wait_recv()
        copy_y(k).start()
        if relay:

            @pl.when(parity == 1)
            def _():
                copy_x(k, inbox).start()
        else:
            copy_x(k, inbox).start()

    def stage_b(k):
        copy_y(k).wait_recv()
        if relay:

            @pl.when(parity == 0)
            def _():
                copy_x(k, ybox).start()

    def patches(at):
        own = inbox[at].astype(F32)
        ore = own[:, :BLK]
        oim = own[:, BLK:]
        tops = []
        lows = []
        for box in (xbox, ybox):
            oth = box[at].astype(F32)
            tre = oth[:, :BLK]
            tim = oth[:, BLK:]
            tops.append(ore * tre + oim * tim)
            lows.append(oim * tre - ore * tim)
        pair = jnp.concatenate(
            [jnp.concatenate(tops, axis=1), jnp.concatenate(lows, axis=1)], axis=0
        ).astype(BF)

        def turned(x):
            return jnp.concatenate(
                [
                    jnp.concatenate([x[:BLK, :BLK], x[BLK:, :BLK]], axis=1),
                    jnp.concatenate([x[:BLK, BLK:], x[BLK:, BLK:]], axis=1),
                ],
                axis=0,
            )

        rows = mm(gfl_ref[...], pair).astype(BF)
        spectrum = mm(turned(rows), gfr_ref[...])
        weighted = []
        for x in range(2):
            spec = spectrum[x * BLK : (x + 1) * BLK]
            sre = spec[:, :BLK]
            sim = spec[:, BLK:]
            power = sre * sre + sim * sim
            line = power + pltpu.roll(power, 1, 1) + pltpu.roll(power, BLK - 1, 1)
            smooth = (line + pltpu.roll(line, 1, 0) + pltpu.roll(line, BLK - 1, 0)) * (1.0 / 9.0)
            level = jnp.sum(jnp.sum(smooth, axis=0, keepdims=True), axis=1, keepdims=True)
            level = level * (1.0 / (BLK * BLK)) + 1e-06
            weight = lax.rsqrt(lax.rsqrt(smooth * (1.0 / level)))
            weighted.append(jnp.concatenate([sre * weight, sim * weight], axis=1))
        weighted = jnp.concatenate(weighted, axis=0).astype(BF)
        back = mm(gbl_ref[...], turned(weighted)).astype(BF)
        done = mm(turned(back), gbr_ref[...]).astype(BF)
        for x in range(2):
            for c in range(2):
                fil[at, x, c] = done[x * BLK : (x + 1) * BLK, c * BLK : (c + 1) * BLK]

    def stage_c(k):
        copy_x(k, inbox).wait_recv()
        patches(k)

    def many(stage, first, stop):
        def one(k, _):
            stage(k)
            return 0

        lax.fori_loop(first, stop, one, 0)

    for e in range(most):
        stage_a(e)
    many(stage_a, most, 4)
    many(stage_b, 0, 2)
    many(stage_a, 4, 6)
    many(stage_b, 2, 4)
    many(stage_a, 6, 8)

    def opening(e, _):
        stage_c(e)
        stage_b(e + 4)
        return 0

    lax.fori_loop(0, 2, opening, 0)
    stage_b(6)

    def step(e, _):
        stage_c(e - 6)
        stage_b(e - 1)
        stage_a(e)
        return 0

    lax.fori_loop(8, total, step, 0)
    many(stage_c, total - 6, total - 3)
    stage_b(total - 1)
    many(stage_c, total - 3, total)

    def drain(k, _):
        copy_y(k).wait_send()
        copy_x(k, inbox).wait_send()
        return 0

    def drain_one(k, _):
        copy_one(k).wait_send()
        return 0

    def drain_two(k, _):
        copy_two(k).wait_send()
        return 0

    lax.fori_loop(1, n, drain_one, 0)
    lax.fori_loop(most, total, drain_two, 0)
    lax.fori_loop(0, total, drain, 0)


def place(capacity, entry_ref, fil, out_ref, sems):
    def copy(q):
        return pltpu.make_async_copy(fil.at[entry_ref[q]], out_ref.at[q], sems.at[q])

    for q in range(capacity):
        copy(q).start()
    for q in range(capacity):
        copy(q).wait()


def body(dates, echo_spectra, range_reference, azimuth_reference, block_owner, block_slot, kernel_index):
    n = lax.axis_size("shard")
    most = max(2, 2 * BLK_DEV // n)
    capacity = min(2 * BLK_DEV, n * most)
    echo = echo_spectra[0]
    pulses, rng = echo.shape[1:]
    inner = rng // BLK
    mine = rng // BLK // n
    wide = pulses * n
    tables = [
        first_table(rng),
        twiddle_table(rng),
        left_table(inner, 1),
        left_table(wide, -1),
        left_table(wide, 1),
        kernel_table(),
        left_table(BLK, -1),
        right_table(BLK, -1),
        left_table(BLK, 1),
        right_table(BLK, 1),
    ]
    smem = pl.BlockSpec(memory_space=pltpu.SMEM)
    vmem = pl.BlockSpec(memory_space=pltpu.VMEM)
    box = pltpu.VMEM((n * most, BLK, 2 * BLK), BF)
    sems = pltpu.SemaphoreType.DMA((n,))
    filtered, entry = pl.pallas_call(
        functools.partial(kernel, n, dates, most, capacity),
        out_shape=(
            jax.ShapeDtypeStruct((n * most + 1, 2, 2, BLK, BLK), BF),
            jax.ShapeDtypeStruct((capacity,), jnp.int32),
        ),
        in_specs=[smem] * 3 + [vmem] * 13,
        out_specs=(vmem, smem),
        scratch_shapes=[
            pltpu.SMEM((n * most,), jnp.int32),
            pltpu.SMEM((n * most,), jnp.int32),
            pltpu.VMEM((pulses * inner, 2 * BLK), BF),
            pltpu.VMEM((2, pulses, rng // BLK, BLK), F32),
            pltpu.VMEM((2, rng // BLK, pulses, BLK), BF),
            pltpu.VMEM((2, mine, wide, BLK), BF),
            pltpu.VMEM((BLK_DEV, BLK, 2 * BLK), BF),
            box,
            box,
            box,
            box,
            sems,
            sems,
            *[pltpu.SemaphoreType.DMA((n * most,))] * 6,
        ],
        compiler_params=pltpu.CompilerParams(collective_id=0, has_side_effects=True, vmem_limit_bytes=(12 + n * most // 2) << 20),
    )(
        block_owner,
        block_slot,
        kernel_index,
        echo,
        range_reference,
        azimuth_reference,
        *[jnp.asarray(t) for t in tables],
    )
    out = pl.pallas_call(
        functools.partial(place, capacity),
        out_shape=jax.ShapeDtypeStruct((capacity, 2, 2, BLK, BLK), BF),
        in_specs=[smem, vmem],
        out_specs=pl.BlockSpec(memory_space=pl.ANY),
        scratch_shapes=[pltpu.SemaphoreType.DMA((capacity,))],
        compiler_params=pltpu.CompilerParams(vmem_limit_bytes=8 << 20),
    )(entry, filtered)
    return out[None]


def solution(mesh):
    in_specs = (
        P(("grp", "date"), None, "shard", None),
        P(),
        P(None, None, "shard"),
        P(("grp", "date"), None),
        P(("grp", "date"), None),
        P(("grp", "date"), None),
    )
    out_specs = P(("grp", "date"), "shard", None, None, None, None)
    return jax.shard_map(
        functools.partial(body, mesh.shape["date"]),
        mesh=mesh,
        in_specs=in_specs,
        out_specs=out_specs,
        check_vma=False,
    )
```

```python
import functools
import math

import jax
import jax.numpy as jnp
import ml_dtypes
import numpy as np
from jax import lax
from jax.experimental import pallas as pl
from jax.experimental.pallas import tpu as pltpu
from jax.sharding import PartitionSpec as P

BLK = 128
NSUB = 8
BLK_DEV = 8
BF = jnp.bfloat16
F32 = jnp.float32


def dft_parts(size, sign):
    index = np.arange(size)
    angle = 2.0 * math.pi / size * (index[:, None] * index[None, :] % size)
    scale = 1.0 / math.sqrt(size)
    return np.cos(angle) * scale, sign * np.sin(angle) * scale


def left_table(size, sign):
    cosine, sine = dft_parts(size, sign)
    return np.block([[cosine, -sine], [sine, cosine]]).astype(ml_dtypes.bfloat16)


def right_table(size, sign):
    return np.ascontiguousarray(left_table(size, sign).T)


def first_table(rng):
    outer, inner = BLK, rng // BLK
    low = outer * BLK // rng
    cosine, sine = dft_parts(outer, 1)
    full = np.stack([np.stack([cosine, sine], 1), np.stack([-sine, cosine], 1)])
    full = full.reshape(2, outer // low, low, 2 * outer)
    return np.transpose(full, (2, 0, 1, 3)).reshape(2 * outer, 2 * outer).astype(ml_dtypes.bfloat16)


def twiddle_table(rng):
    inner = rng // BLK
    phase = np.arange(inner)[:, None] * np.arange(BLK)[None, :] % rng
    angle = 2.0 * math.pi / rng * phase
    return np.stack([np.cos(angle), np.sin(angle)]).astype(np.float32)


def kernel_table():
    offset = (np.arange(NSUB) + 0.5) / NSUB
    cells = np.arange(BLK)
    dist = cells[None, None, :] - cells[None, :, None] - offset[:, None, None]
    window = np.where(np.abs(dist) < 4.0, 0.5 + 0.5 * np.cos(math.pi * dist / 4.0), 0.0)
    return (np.sinc(dist) * window).astype(ml_dtypes.bfloat16)


def flipped(a, b, n):
    total = 0
    bit = 1
    while bit < n:
        total = total + (a // bit + b // bit) % 2 * bit
        bit *= 2
    return total


def mm(left, right):
    return jnp.dot(left, right, preferred_element_type=F32)


def kernel(
    n,
    dates,
    most,
    capacity,
    owner_hbm,
    slot_hbm,
    kinds_hbm,
    echo_hbm,
    rref_hbm,
    aref_hbm,
    t1_hbm,
    tw_hbm,
    w2_hbm,
    pf_hbm,
    pb_hbm,
    kt_hbm,
    gfl_hbm,
    gfr_hbm,
    gbl_hbm,
    gbr_hbm,
    fil_hbm,
    entry_ref,
    fil,
    src_ref,
    kind_ref,
    lhs,
    mat,
    snd,
    cols,
    blocks,
    outbox,
    inbox,
    ybox,
    xbox,
    sw,
    owner_ref,
    slot_ref,
    kinds_ref,
    echo_ref,
    rref_ref,
    aref_ref,
    t1_ref,
    tw_ref,
    w2_ref,
    pf_ref,
    pb_ref,
    kt_ref,
    gfl_ref,
    gfr_ref,
    gbl_ref,
    gbr_ref,
    s0,
    s1,
    r1,
    s2,
    r2,
    sy,
    ry,
    sx,
    rx,
):
    loads = [
        pltpu.make_async_copy(source, held, s0.at[at])
        for at, (source, held) in enumerate(
            [
                (echo_hbm, echo_ref),
                (rref_hbm, rref_ref),
                (t1_hbm, t1_ref),
                (tw_hbm, tw_ref),
                (w2_hbm, w2_ref),
                (owner_hbm, owner_ref),
                (slot_hbm, slot_ref),
                (kinds_hbm, kinds_ref),
                (pf_hbm, pf_ref),
                (aref_hbm, aref_ref),
                (pb_hbm, pb_ref),
                (kt_hbm, kt_ref),
                (gfl_hbm, gfl_ref),
                (gfr_hbm, gfr_ref),
                (gbl_hbm, gbl_ref),
                (gbr_hbm, gbr_ref),
            ]
        )
    ]
    for load in loads:
        load.start()
    me = lax.axis_index("shard")
    day = lax.axis_index("date")
    grp = lax.axis_index("grp")
    relay = dates == 4
    ydst = lax.rem(day + dates - 2, dates)
    if relay:
        parity = lax.rem(day, 2)
        xdst = day + 1 - 2 * parity
        xsrc = xdst
    else:
        xdst = lax.rem(day + dates - 1, dates)
        xsrc = lax.rem(day + 1, dates)
    ysrc = lax.rem(day + 2, dates)
    mesh_id = pl.DeviceIdType.MESH

    barrier = pltpu.get_barrier_semaphore()

    def greet(k, _):
        pl.semaphore_signal(
            barrier, inc=1, device_id=(grp, day, flipped(me, k, n)), device_id_type=mesh_id
        )
        return 0

    lax.fori_loop(1, n, greet, 0)
    for other in (ysrc, xsrc):
        pl.semaphore_signal(barrier, inc=1, device_id=(grp, other, me), device_id_type=mesh_id)

    pulses = echo_ref.shape[1]
    rng = echo_ref.shape[2]
    tiles = rng // BLK
    inner = rng // BLK
    mine = tiles // n
    wide = n * pulses

    loads[0].wait()
    loads[1].wait()
    real = echo_ref[0].astype(F32)
    imag = echo_ref[1].astype(F32)
    rre = rref_ref[0:1, :]
    rim = rref_ref[1:2, :]
    mat[0] = (real * rre + imag * rim).reshape(pulses, tiles, BLK)
    mat[1] = (imag * rre - real * rim).reshape(pulses, tiles, BLK)

    for p in range(pulses):
        both = jnp.concatenate([mat[0, p], mat[1, p]], axis=0).T
        low = BLK // inner
        parts = [both[x * inner : (x + 1) * inner] for x in range(low)]
        lhs[p * inner : (p + 1) * inner, :] = jnp.concatenate(parts, axis=1).astype(BF)

    for load in loads[2:5]:
        load.wait()
    twc = tw_ref[0]
    tws = tw_ref[1]
    group = 4
    for g in range(0, pulses, group):
        section = mm(lhs[g * inner : (g + group) * inner, :], t1_ref[...])
        rights = []
        for p in range(group):
            sre = section[p * inner : (p + 1) * inner, :BLK]
            sim = section[p * inner : (p + 1) * inner, BLK:]
            rights.append(
                jnp.concatenate([sre * twc - sim * tws, sre * tws + sim * twc], axis=0).astype(BF)
            )
        second = mm(w2_ref[...], jnp.concatenate(rights, axis=1))
        for p in range(group):
            mat[:, g + p] = second[:, p * BLK : (p + 1) * BLK].reshape(2, tiles, BLK)
    for c in range(2):
        snd[c] = jnp.swapaxes(mat[c], 0, 1).astype(BF)

    pl.semaphore_wait(barrier, n + 1)

    def copy_one(k):
        dest = flipped(me, k, n)
        return pltpu.make_async_remote_copy(
            src_ref=snd.at[:, pl.ds(dest * mine, mine)],
            dst_ref=cols.at[:, :, pl.ds(me * pulses, pulses)],
            send_sem=s1.at[k],
            recv_sem=r1.at[k],
            device_id=(grp, day, dest),
            device_id_type=mesh_id,
        )

    def wait_one(k):
        source = flipped(me, k, n)
        return pltpu.make_async_remote_copy(
            src_ref=snd.at[:, pl.ds(me * mine, mine)],
            dst_ref=cols.at[:, :, pl.ds(source * pulses, pulses)],
            send_sem=s1.at[k],
            recv_sem=r1.at[k],
            device_id=(grp, day, source),
            device_id_type=mesh_id,
        )

    def start_one(k, _):
        copy_one(k).start()
        return 0

    def end_one(k, _):
        wait_one(k).wait_recv()
        return 0

    lax.fori_loop(1, n, start_one, 0)
    cols[:, :, pl.ds(me * pulses, pulses)] = snd[:, pl.ds(me * mine, mine)]

    for load in loads[5:]:
        load.wait()

    def sources(k, _):
        dest = flipped(me, k, n)
        seen = jnp.int32(0)
        found = [jnp.int32(0)] * most
        for b in range(BLK_DEV):
            named = owner_ref[0, me * BLK_DEV + b] == dest
            for r in range(most):
                found[r] = jnp.where(named & (seen == r), b, found[r])
            seen = seen + named.astype(jnp.int32)
        for r in range(most):
            src_ref[k * most + r] = found[r]
            kind_ref[k * most + r] = kinds_ref[0, me * BLK_DEV + found[r]]
        return 0

    lax.fori_loop(0, n, sources, 0)

    def entries(t, held):
        held = list(held)
        at = flipped(me, t, n) * most
        for b in range(BLK_DEV):
            named = owner_ref[0, t * BLK_DEV + b] == me
            slot = jnp.where(named, slot_ref[0, t * BLK_DEV + b], -1)
            for q in range(capacity):
                held[q] = jnp.where(slot == q, at, held[q])
            at = at + named.astype(jnp.int32)
        return tuple(held)

    held = lax.fori_loop(0, n, entries, (jnp.int32(n * most),) * capacity)
    for q in range(capacity):
        entry_ref[q] = held[q]
    fil[n * most] = jnp.zeros_like(fil[n * most])

    def write(e):
        return pltpu.make_async_copy(fil.at[e], fil_hbm.at[e], sw.at[e])

    write(n * most).start()
    lax.fori_loop(1, n, end_one, 0)

    rows_of = wide // BLK
    for j in range(0, mine, 2):
        right = jnp.concatenate(
            [
                jnp.concatenate([cols[0, j], cols[1, j]], axis=0),
                jnp.concatenate([cols[0, j + 1], cols[1, j + 1]], axis=0),
            ],
            axis=1,
        )
        doppler = mm(pf_ref[...], right)
        are = aref_ref[0, :, j * BLK : (j + 2) * BLK].astype(F32)
        aim = aref_ref[1, :, j * BLK : (j + 2) * BLK].astype(F32)
        dre = doppler[:wide]
        dim = doppler[wide:]
        shaped = jnp.concatenate([dre * are - dim * aim, dre * aim + dim * are], axis=0).astype(BF)
        image = mm(pb_ref[...], shaped).astype(BF)
        for x in range(2):
            for y in range(rows_of):
                for c in range(2):
                    low = c * wide + y * BLK
                    blocks[y * mine + j + x, :, c * BLK : (c + 1) * BLK] = image[
                        low : low + BLK, x * BLK : (x + 1) * BLK
                    ]

    def resampled(at):
        return mm(kt_ref[kind_ref[at]], blocks[src_ref[at]]).astype(BF)

    total = n * most
    for e in range(most):
        inbox[e] = resampled(e)

    def copy_two(e):
        return pltpu.make_async_remote_copy(
            src_ref=outbox.at[e],
            dst_ref=inbox.at[e],
            send_sem=s2.at[e],
            recv_sem=r2.at[e],
            device_id=(grp, day, flipped(me, e // most, n)),
            device_id_type=mesh_id,
        )

    def start_two(e, _):
        outbox[e] = resampled(e)
        copy_two(e).start()
        return 0

    lax.fori_loop(most, total, start_two, 0)

    def copy_y(k):
        return pltpu.make_async_remote_copy(
            src_ref=inbox.at[k],
            dst_ref=ybox.at[k],
            send_sem=sy.at[k],
            recv_sem=ry.at[k],
            device_id=(grp, ydst, me),
            device_id_type=mesh_id,
        )

    def copy_x(k, source):
        return pltpu.make_async_remote_copy(
            src_ref=source.at[k],
            dst_ref=xbox.at[k],
            send_sem=sx.at[k],
            recv_sem=rx.at[k],
            device_id=(grp, xdst, me),
            device_id_type=mesh_id,
        )

    def stage_a(k):
        if not isinstance(k, int) or k >= most:
            copy_two(k).wait_recv()
        copy_y(k).start()
        if relay:

            @pl.when(parity == 1)
            def _():
                copy_x(k, inbox).start()
        else:
            copy_x(k, inbox).start()

    def stage_b(k):
        copy_y(k).wait_recv()
        if relay:

            @pl.when(parity == 0)
            def _():
                copy_x(k, ybox).start()

    def patches(at):
        own = inbox[at].astype(F32)
        ore = own[:, :BLK]
        oim = own[:, BLK:]
        tops = []
        lows = []
        for box in (xbox, ybox):
            oth = box[at].astype(F32)
            tre = oth[:, :BLK]
            tim = oth[:, BLK:]
            tops.append(ore * tre + oim * tim)
            lows.append(oim * tre - ore * tim)
        pair = jnp.concatenate(
            [jnp.concatenate(tops, axis=1), jnp.concatenate(lows, axis=1)], axis=0
        ).astype(BF)

        def turned(x):
            return jnp.concatenate(
                [
                    jnp.concatenate([x[:BLK, :BLK], x[BLK:, :BLK]], axis=1),
                    jnp.concatenate([x[:BLK, BLK:], x[BLK:, BLK:]], axis=1),
                ],
                axis=0,
            )

        rows = mm(gfl_ref[...], pair).astype(BF)
        spectrum = mm(turned(rows), gfr_ref[...])
        weighted = []
        for x in range(2):
            spec = spectrum[x * BLK : (x + 1) * BLK]
            sre = spec[:, :BLK]
            sim = spec[:, BLK:]
            power = sre * sre + sim * sim
            line = power + pltpu.roll(power, 1, 1) + pltpu.roll(power, BLK - 1, 1)
            smooth = (line + pltpu.roll(line, 1, 0) + pltpu.roll(line, BLK - 1, 0)) * (1.0 / 9.0)
            level = jnp.sum(jnp.sum(smooth, axis=0, keepdims=True), axis=1, keepdims=True)
            level = level * (1.0 / (BLK * BLK)) + 1e-06
            weight = lax.rsqrt(lax.rsqrt(smooth * (1.0 / level)))
            weighted.append(jnp.concatenate([sre * weight, sim * weight], axis=1))
        weighted = jnp.concatenate(weighted, axis=0).astype(BF)
        back = mm(gbl_ref[...], turned(weighted)).astype(BF)
        done = mm(turned(back), gbr_ref[...]).astype(BF)
        for x in range(2):
            for c in range(2):
                fil[at, x, c] = done[x * BLK : (x + 1) * BLK, c * BLK : (c + 1) * BLK]

    def stage_c(k):
        copy_x(k, inbox).wait_recv()
        patches(k)
        write(k).start()

    def many(stage, first, stop):
        def one(k, _):
            stage(k)
            return 0

        lax.fori_loop(first, stop, one, 0)

    for e in range(most):
        stage_a(e)
    many(stage_a, most, 4)

    def opening(e, _):
        stage_a(e + 4)
        stage_b(e)
        return 0

    lax.fori_loop(0, 4, opening, 0)

    def middle(e, _):
        stage_c(e)
        stage_b(e + 4)
        return 0

    lax.fori_loop(0, 3, middle, 0)

    def step(e, _):
        stage_a(e)
        stage_b(e - 1)
        stage_c(e - 5)
        return 0

    lax.fori_loop(8, total, step, 0)
    many(stage_c, total - 5, total - 3)
    stage_b(total - 1)
    many(stage_c, total - 3, total)

    def drain(k, _):
        copy_y(k).wait_send()
        copy_x(k, inbox).wait_send()
        return 0

    def drain_one(k, _):
        copy_one(k).wait_send()
        return 0

    def drain_two(k, _):
        copy_two(k).wait_send()
        return 0

    lax.fori_loop(1, n, drain_one, 0)
    lax.fori_loop(most, total, drain_two, 0)
    lax.fori_loop(0, total, drain, 0)

    def written(k, _):
        write(k).wait()
        return 0

    lax.fori_loop(0, total + 1, written, 0)


def place(capacity, entry_ref, fil, out_ref, held, near, far):
    def take(q):
        return pltpu.make_async_copy(fil.at[entry_ref[q]], held.at[q], near.at[q])

    def give(q):
        return pltpu.make_async_copy(held.at[q], out_ref.at[q], far.at[q])

    for q in range(capacity):
        take(q).start()
    for q in range(capacity):
        take(q).wait()
        give(q).start()
    for q in range(capacity):
        give(q).wait()


def body(dates, echo_spectra, range_reference, azimuth_reference, block_owner, block_slot, kernel_index):
    n = lax.axis_size("shard")
    most = max(2, 2 * BLK_DEV // n)
    capacity = min(2 * BLK_DEV, n * most)
    echo = echo_spectra[0]
    pulses, rng = echo.shape[1:]
    inner = rng // BLK
    mine = rng // BLK // n
    wide = pulses * n
    tables = [
        first_table(rng),
        twiddle_table(rng),
        left_table(inner, 1),
        left_table(wide, -1),
        left_table(wide, 1),
        kernel_table(),
        left_table(BLK, -1),
        right_table(BLK, -1),
        left_table(BLK, 1),
        right_table(BLK, 1),
    ]
    smem = pl.BlockSpec(memory_space=pltpu.SMEM)
    hbm = pl.BlockSpec(memory_space=pl.ANY)
    box = pltpu.VMEM((n * most, BLK, 2 * BLK), BF)
    sems = pltpu.SemaphoreType.DMA((n,))
    tables = [jnp.asarray(t) for t in tables]
    operands = [block_owner, block_slot, kernel_index, echo, range_reference, azimuth_reference]
    operands += tables
    filtered, entry = pl.pallas_call(
        functools.partial(kernel, n, dates, most, capacity),
        out_shape=(
            jax.ShapeDtypeStruct((n * most + 1, 2, 2, BLK, BLK), BF),
            jax.ShapeDtypeStruct((capacity,), jnp.int32),
        ),
        in_specs=[hbm] * 16,
        out_specs=(hbm, smem),
        scratch_shapes=[
            pltpu.VMEM((n * most + 1, 2, 2, BLK, BLK), BF),
            pltpu.SMEM((n * most,), jnp.int32),
            pltpu.SMEM((n * most,), jnp.int32),
            pltpu.VMEM((pulses * inner, 2 * BLK), BF),
            pltpu.VMEM((2, pulses, rng // BLK, BLK), F32),
            pltpu.VMEM((2, rng // BLK, pulses, BLK), BF),
            pltpu.VMEM((2, mine, wide, BLK), BF),
            pltpu.VMEM((BLK_DEV, BLK, 2 * BLK), BF),
            box,
            box,
            box,
            box,
            pltpu.SemaphoreType.DMA((n * most + 1,)),
            *[pltpu.SMEM(x.shape, x.dtype) for x in operands[:3]],
            *[pltpu.VMEM(x.shape, x.dtype) for x in operands[3:]],
            pltpu.SemaphoreType.DMA((len(operands),)),
            sems,
            sems,
            *[pltpu.SemaphoreType.DMA((n * most,))] * 6,
        ],
        compiler_params=pltpu.CompilerParams(collective_id=0, has_side_effects=True),
    )(
        *operands
    )
    out = pl.pallas_call(
        functools.partial(place, capacity),
        out_shape=jax.ShapeDtypeStruct((capacity, 2, 2, BLK, BLK), BF),
        in_specs=[smem, hbm],
        out_specs=pl.BlockSpec(memory_space=pl.ANY),
        scratch_shapes=[
            pltpu.VMEM((capacity, 2, 2, BLK, BLK), BF),
            *[pltpu.SemaphoreType.DMA((capacity,))] * 2,
        ],
    )(entry, filtered)
    return out[None]


def solution(mesh):
    in_specs = (
        P(("grp", "date"), None, "shard", None),
        P(),
        P(None, None, "shard"),
        P(("grp", "date"), None),
        P(("grp", "date"), None),
        P(("grp", "date"), None),
    )
    out_specs = P(("grp", "date"), "shard", None, None, None, None)
    return jax.shard_map(
        functools.partial(body, mesh.shape["date"]),
        mesh=mesh,
        in_specs=in_specs,
        out_specs=out_specs,
        check_vma=False,
    )
```

```python
import functools
import math

import jax
import jax.numpy as jnp
import ml_dtypes
import numpy as np
from jax import lax
from jax.experimental import pallas as pl
from jax.experimental.pallas import tpu as pltpu
from jax.sharding import PartitionSpec as P

BLK = 128
NSUB = 8
BLK_DEV = 8
BF = jnp.bfloat16
F32 = jnp.float32


def dft_parts(size, sign):
    index = np.arange(size)
    angle = 2.0 * math.pi / size * (index[:, None] * index[None, :] % size)
    scale = 1.0 / math.sqrt(size)
    return np.cos(angle) * scale, sign * np.sin(angle) * scale


def left_table(size, sign):
    cosine, sine = dft_parts(size, sign)
    return np.block([[cosine, -sine], [sine, cosine]]).astype(ml_dtypes.bfloat16)


def right_table(size, sign):
    return np.ascontiguousarray(left_table(size, sign).T)


def first_table(rng):
    outer, inner = BLK, rng // BLK
    low = outer * BLK // rng
    cosine, sine = dft_parts(outer, 1)
    full = np.stack([np.stack([cosine, sine], 1), np.stack([-sine, cosine], 1)])
    full = full.reshape(2, outer // low, low, 2 * outer)
    return np.transpose(full, (2, 0, 1, 3)).reshape(2 * outer, 2 * outer).astype(ml_dtypes.bfloat16)


def twiddle_table(rng):
    inner = rng // BLK
    phase = np.arange(inner)[:, None] * np.arange(BLK)[None, :] % rng
    angle = 2.0 * math.pi / rng * phase
    return np.stack([np.cos(angle), np.sin(angle)]).astype(np.float32)


def kernel_table():
    offset = (np.arange(NSUB) + 0.5) / NSUB
    cells = np.arange(BLK)
    dist = cells[None, None, :] - cells[None, :, None] - offset[:, None, None]
    window = np.where(np.abs(dist) < 4.0, 0.5 + 0.5 * np.cos(math.pi * dist / 4.0), 0.0)
    return (np.sinc(dist) * window).astype(ml_dtypes.bfloat16)


def flipped(a, b, n):
    total = 0
    bit = 1
    while bit < n:
        total = total + (a // bit + b // bit) % 2 * bit
        bit *= 2
    return total


def mm(left, right):
    return jnp.dot(left, right, preferred_element_type=F32)


def kernel(
    n,
    dates,
    most,
    capacity,
    owner_ref,
    slot_ref,
    kinds_ref,
    echo_ref,
    rref_ref,
    aref_ref,
    t1_ref,
    tw_ref,
    w2_ref,
    pf_ref,
    pb_ref,
    kt_ref,
    gfl_ref,
    gfr_ref,
    gbl_ref,
    gbr_ref,
    fil_hbm,
    entry_ref,
    fil,
    src_ref,
    kind_ref,
    lhs,
    mat,
    snd,
    cols,
    blocks,
    outbox,
    inbox,
    ybox,
    xbox,
    sw,
    s1,
    r1,
    s2,
    r2,
    sy,
    ry,
    sx,
    rx,
):
    me = lax.axis_index("shard")
    day = lax.axis_index("date")
    grp = lax.axis_index("grp")
    relay = dates == 4
    ydst = lax.rem(day + dates - 2, dates)
    if relay:
        parity = lax.rem(day, 2)
        xdst = day + 1 - 2 * parity
        xsrc = xdst
    else:
        xdst = lax.rem(day + dates - 1, dates)
        xsrc = lax.rem(day + 1, dates)
    ysrc = lax.rem(day + 2, dates)
    mesh_id = pl.DeviceIdType.MESH

    barrier = pltpu.get_barrier_semaphore()

    def greet(k, _):
        pl.semaphore_signal(
            barrier, inc=1, device_id=(grp, day, flipped(me, k, n)), device_id_type=mesh_id
        )
        return 0

    lax.fori_loop(1, n, greet, 0)
    for other in (ysrc, xsrc):
        pl.semaphore_signal(barrier, inc=1, device_id=(grp, other, me), device_id_type=mesh_id)

    pulses = echo_ref.shape[1]
    rng = echo_ref.shape[2]
    tiles = rng // BLK
    inner = rng // BLK
    mine = tiles // n
    wide = n * pulses

    real = echo_ref[0].astype(F32)
    imag = echo_ref[1].astype(F32)
    rre = rref_ref[0:1, :]
    rim = rref_ref[1:2, :]
    mat[0] = (real * rre + imag * rim).reshape(pulses, tiles, BLK)
    mat[1] = (imag * rre - real * rim).reshape(pulses, tiles, BLK)

    for p in range(pulses):
        both = jnp.concatenate([mat[0, p], mat[1, p]], axis=0).T
        low = BLK // inner
        parts = [both[x * inner : (x + 1) * inner] for x in range(low)]
        lhs[p * inner : (p + 1) * inner, :] = jnp.concatenate(parts, axis=1).astype(BF)

    twc = tw_ref[0]
    tws = tw_ref[1]
    group = 4
    for g in range(0, pulses, group):
        section = mm(lhs[g * inner : (g + group) * inner, :], t1_ref[...])
        rights = []
        for p in range(group):
            sre = section[p * inner : (p + 1) * inner, :BLK]
            sim = section[p * inner : (p + 1) * inner, BLK:]
            rights.append(
                jnp.concatenate([sre * twc - sim * tws, sre * tws + sim * twc], axis=0).astype(BF)
            )
        second = mm(w2_ref[...], jnp.concatenate(rights, axis=1))
        for p in range(group):
            mat[:, g + p] = second[:, p * BLK : (p + 1) * BLK].reshape(2, tiles, BLK)
    for c in range(2):
        snd[c] = jnp.swapaxes(mat[c], 0, 1).astype(BF)

    pl.semaphore_wait(barrier, n + 1)

    def copy_one(k):
        dest = flipped(me, k, n)
        return pltpu.make_async_remote_copy(
            src_ref=snd.at[:, pl.ds(dest * mine, mine)],
            dst_ref=cols.at[:, :, pl.ds(me * pulses, pulses)],
            send_sem=s1.at[k],
            recv_sem=r1.at[k],
            device_id=(grp, day, dest),
            device_id_type=mesh_id,
        )

    def wait_one(k):
        source = flipped(me, k, n)
        return pltpu.make_async_remote_copy(
            src_ref=snd.at[:, pl.ds(me * mine, mine)],
            dst_ref=cols.at[:, :, pl.ds(source * pulses, pulses)],
            send_sem=s1.at[k],
            recv_sem=r1.at[k],
            device_id=(grp, day, source),
            device_id_type=mesh_id,
        )

    def start_one(k, _):
        copy_one(k).start()
        return 0

    def end_one(k, _):
        wait_one(k).wait_recv()
        return 0

    lax.fori_loop(1, n, start_one, 0)
    cols[:, :, pl.ds(me * pulses, pulses)] = snd[:, pl.ds(me * mine, mine)]

    def sources(k, _):
        dest = flipped(me, k, n)
        seen = jnp.int32(0)
        found = [jnp.int32(0)] * most
        for b in range(BLK_DEV):
            named = owner_ref[0, me * BLK_DEV + b] == dest
            for r in range(most):
                found[r] = jnp.where(named & (seen == r), b, found[r])
            seen = seen + named.astype(jnp.int32)
        for r in range(most):
            src_ref[k * most + r] = found[r]
            kind_ref[k * most + r] = kinds_ref[0, me * BLK_DEV + found[r]]
        return 0

    lax.fori_loop(0, n, sources, 0)

    def entries(t, held):
        held = list(held)
        at = flipped(me, t, n) * most
        for b in range(BLK_DEV):
            named = owner_ref[0, t * BLK_DEV + b] == me
            slot = jnp.where(named, slot_ref[0, t * BLK_DEV + b], -1)
            for q in range(capacity):
                held[q] = jnp.where(slot == q, at, held[q])
            at = at + named.astype(jnp.int32)
        return tuple(held)

    held = lax.fori_loop(0, n, entries, (jnp.int32(n * most),) * capacity)
    for q in range(capacity):
        entry_ref[q] = held[q]
    fil[n * most] = jnp.zeros_like(fil[n * most])

    def write(e):
        return pltpu.make_async_copy(fil.at[e], fil_hbm.at[e], sw.at[e])

    write(n * most).start()
    lax.fori_loop(1, n, end_one, 0)

    rows_of = wide // BLK
    for j in range(0, mine, 2):
        right = jnp.concatenate(
            [
                jnp.concatenate([cols[0, j], cols[1, j]], axis=0),
                jnp.concatenate([cols[0, j + 1], cols[1, j + 1]], axis=0),
            ],
            axis=1,
        )
        doppler = mm(pf_ref[...], right)
        are = aref_ref[0, :, j * BLK : (j + 2) * BLK].astype(F32)
        aim = aref_ref[1, :, j * BLK : (j + 2) * BLK].astype(F32)
        dre = doppler[:wide]
        dim = doppler[wide:]
        shaped = jnp.concatenate([dre * are - dim * aim, dre * aim + dim * are], axis=0).astype(BF)
        image = mm(pb_ref[...], shaped).astype(BF)
        for x in range(2):
            for y in range(rows_of):
                for c in range(2):
                    low = c * wide + y * BLK
                    blocks[y * mine + j + x, :, c * BLK : (c + 1) * BLK] = image[
                        low : low + BLK, x * BLK : (x + 1) * BLK
                    ]

    def resampled(at):
        return mm(kt_ref[kind_ref[at]], blocks[src_ref[at]]).astype(BF)

    total = n * most
    for e in range(most):
        inbox[e] = resampled(e)

    def copy_two(e):
        return pltpu.make_async_remote_copy(
            src_ref=outbox.at[e],
            dst_ref=inbox.at[e],
            send_sem=s2.at[e],
            recv_sem=r2.at[e],
            device_id=(grp, day, flipped(me, e // most, n)),
            device_id_type=mesh_id,
        )

    def start_two(e, _):
        outbox[e] = resampled(e)
        copy_two(e).start()
        return 0

    lax.fori_loop(most, total, start_two, 0)

    def copy_y(k):
        return pltpu.make_async_remote_copy(
            src_ref=inbox.at[k],
            dst_ref=ybox.at[k],
            send_sem=sy.at[k],
            recv_sem=ry.at[k],
            device_id=(grp, ydst, me),
            device_id_type=mesh_id,
        )

    def copy_x(k, source):
        return pltpu.make_async_remote_copy(
            src_ref=source.at[k],
            dst_ref=xbox.at[k],
            send_sem=sx.at[k],
            recv_sem=rx.at[k],
            device_id=(grp, xdst, me),
            device_id_type=mesh_id,
        )

    def stage_a(k):
        if not isinstance(k, int) or k >= most:
            copy_two(k).wait_recv()
        copy_y(k).start()
        if relay:

            @pl.when(parity == 1)
            def _():
                copy_x(k, inbox).start()
        else:
            copy_x(k, inbox).start()

    def stage_b(k):
        copy_y(k).wait_recv()
        if relay:

            @pl.when(parity == 0)
            def _():
                copy_x(k, ybox).start()

    def patches(at):
        own = inbox[at].astype(F32)
        ore = own[:, :BLK]
        oim = own[:, BLK:]
        tops = []
        lows = []
        for box in (xbox, ybox):
            oth = box[at].astype(F32)
            tre = oth[:, :BLK]
            tim = oth[:, BLK:]
            tops.append(ore * tre + oim * tim)
            lows.append(oim * tre - ore * tim)
        pair = jnp.concatenate(
            [jnp.concatenate(tops, axis=1), jnp.concatenate(lows, axis=1)], axis=0
        ).astype(BF)

        def turned(x):
            return jnp.concatenate(
                [
                    jnp.concatenate([x[:BLK, :BLK], x[BLK:, :BLK]], axis=1),
                    jnp.concatenate([x[:BLK, BLK:], x[BLK:, BLK:]], axis=1),
                ],
                axis=0,
            )

        rows = mm(gfl_ref[...], pair).astype(BF)
        spectrum = mm(turned(rows), gfr_ref[...])
        weighted = []
        for x in range(2):
            spec = spectrum[x * BLK : (x + 1) * BLK]
            sre = spec[:, :BLK]
            sim = spec[:, BLK:]
            power = sre * sre + sim * sim
            line = power + pltpu.roll(power, 1, 1) + pltpu.roll(power, BLK - 1, 1)
            smooth = (line + pltpu.roll(line, 1, 0) + pltpu.roll(line, BLK - 1, 0)) * (1.0 / 9.0)
            level = jnp.sum(jnp.sum(smooth, axis=0, keepdims=True), axis=1, keepdims=True)
            level = level * (1.0 / (BLK * BLK)) + 1e-06
            weight = lax.rsqrt(lax.rsqrt(smooth * (1.0 / level)))
            weighted.append(jnp.concatenate([sre * weight, sim * weight], axis=1))
        weighted = jnp.concatenate(weighted, axis=0).astype(BF)
        back = mm(gbl_ref[...], turned(weighted)).astype(BF)
        done = mm(turned(back), gbr_ref[...]).astype(BF)
        for x in range(2):
            for c in range(2):
                fil[at, x, c] = done[x * BLK : (x + 1) * BLK, c * BLK : (c + 1) * BLK]

    def stage_c(k):
        copy_x(k, inbox).wait_recv()
        patches(k)
        write(k).start()

    def many(stage, first, stop):
        def one(k, _):
            stage(k)
            return 0

        lax.fori_loop(first, stop, one, 0)

    for e in range(most):
        stage_a(e)
    many(stage_a, most, 4)

    def opening(e, _):
        stage_a(e + 4)
        stage_b(e)
        return 0

    lax.fori_loop(0, 4, opening, 0)

    def middle(e, _):
        stage_c(e)
        stage_b(e + 4)
        return 0

    lax.fori_loop(0, 2, middle, 0)
    stage_c(2)

    def step(e, _):
        stage_a(e)
        stage_b(e - 2)
        stage_c(e - 5)
        return 0

    lax.fori_loop(8, total, step, 0)
    stage_b(total - 2)
    stage_c(total - 5)
    stage_b(total - 1)
    many(stage_c, total - 4, total)

    def drain(k, _):
        copy_y(k).wait_send()
        copy_x(k, inbox).wait_send()
        return 0

    def drain_one(k, _):
        copy_one(k).wait_send()
        return 0

    def drain_two(k, _):
        copy_two(k).wait_send()
        return 0

    lax.fori_loop(1, n, drain_one, 0)
    lax.fori_loop(most, total, drain_two, 0)
    lax.fori_loop(0, total, drain, 0)

    def written(k, _):
        write(k).wait()
        return 0

    lax.fori_loop(0, total + 1, written, 0)


def place(capacity, entry_ref, fil, out_ref, sems):
    def copy(q):
        return pltpu.make_async_copy(fil.at[entry_ref[q]], out_ref.at[q], sems.at[q])

    for q in range(capacity):
        copy(q).start()
    for q in range(capacity):
        copy(q).wait()


def body(dates, echo_spectra, range_reference, azimuth_reference, block_owner, block_slot, kernel_index):
    n = lax.axis_size("shard")
    most = max(2, 2 * BLK_DEV // n)
    capacity = min(2 * BLK_DEV, n * most)
    echo = echo_spectra[0]
    pulses, rng = echo.shape[1:]
    inner = rng // BLK
    mine = rng // BLK // n
    wide = pulses * n
    tables = [
        first_table(rng),
        twiddle_table(rng),
        left_table(inner, 1),
        left_table(wide, -1),
        left_table(wide, 1),
        kernel_table(),
        left_table(BLK, -1),
        right_table(BLK, -1),
        left_table(BLK, 1),
        right_table(BLK, 1),
    ]
    smem = pl.BlockSpec(memory_space=pltpu.SMEM)
    vmem = pl.BlockSpec(memory_space=pltpu.VMEM)
    hbm = pl.BlockSpec(memory_space=pl.ANY)
    box = pltpu.VMEM((n * most, BLK, 2 * BLK), BF)
    sems = pltpu.SemaphoreType.DMA((n,))
    tables = [jnp.asarray(t) for t in tables]
    operands = [block_owner, block_slot, kernel_index, echo, range_reference, azimuth_reference]
    operands += tables
    filtered, entry = pl.pallas_call(
        functools.partial(kernel, n, dates, most, capacity),
        out_shape=(
            jax.ShapeDtypeStruct((n * most + 1, 2, 2, BLK, BLK), BF),
            jax.ShapeDtypeStruct((capacity,), jnp.int32),
        ),
        in_specs=[smem] * 3 + [vmem] * 13,
        out_specs=(hbm, smem),
        scratch_shapes=[
            pltpu.VMEM((n * most + 1, 2, 2, BLK, BLK), BF),
            pltpu.SMEM((n * most,), jnp.int32),
            pltpu.SMEM((n * most,), jnp.int32),
            pltpu.VMEM((pulses * inner, 2 * BLK), BF),
            pltpu.VMEM((2, pulses, rng // BLK, BLK), F32),
            pltpu.VMEM((2, rng // BLK, pulses, BLK), BF),
            pltpu.VMEM((2, mine, wide, BLK), BF),
            pltpu.VMEM((BLK_DEV, BLK, 2 * BLK), BF),
            box,
            box,
            box,
            box,
            pltpu.SemaphoreType.DMA((n * most + 1,)),
            sems,
            sems,
            *[pltpu.SemaphoreType.DMA((n * most,))] * 6,
        ],
        compiler_params=pltpu.CompilerParams(collective_id=0, has_side_effects=True),
    )(
        *operands
    )
    out = pl.pallas_call(
        functools.partial(place, capacity),
        out_shape=jax.ShapeDtypeStruct((capacity, 2, 2, BLK, BLK), BF),
        in_specs=[smem, vmem],
        out_specs=pl.BlockSpec(memory_space=pl.ANY),
        scratch_shapes=[pltpu.SemaphoreType.DMA((capacity,))],
    )(entry, filtered)
    return out[None]


def solution(mesh):
    in_specs = (
        P(("grp", "date"), None, "shard", None),
        P(),
        P(None, None, "shard"),
        P(("grp", "date"), None),
        P(("grp", "date"), None),
        P(("grp", "date"), None),
    )
    out_specs = P(("grp", "date"), "shard", None, None, None, None)
    return jax.shard_map(
        functools.partial(body, mesh.shape["date"]),
        mesh=mesh,
        in_specs=in_specs,
        out_specs=out_specs,
        check_vma=False,
    )
```
